256 devices in a mesh: wide: 64 (over y, z, core), narrow: 4 (over x).
Axes of the slice: x: 4, y: 4, z: 8, core: 2. Of those that a mesh axis runs over, the one named last changes fastest.
Arguments:
- residual_in: bfloat16 [128, 7168], P('wide', 'narrow'), may hold values from -2 to 2
- query_nope: bfloat16 [128, 64, 128], P('wide', 'narrow'), may hold values from -6 to 6
- query_rope: bfloat16 [128, 64, 64], P('wide', 'narrow'), may hold values from -8 to 8
- absorb_key: bfloat16 [64, 128, 512], P('narrow'), may hold values from -0.5 to 0.5
- absorb_value: bfloat16 [64, 512, 128], P('narrow'), may hold values from -0.25 to 0.25
- latent_cache: bfloat16 [128, 2048, 576], P('wide'), may hold values from -8 to 8
- cache_lengths: int32 [128], P('wide'), may hold values from 256 to 2048, as said below
- slot_rows: int32 [128], replicated, may hold values from 0 to 127, each once
- out_proj: bfloat16 [8192, 7168], P('wide', 'narrow'), may hold values from -0.0625 to 0.0625
- norm_gain: bfloat16 [7168], P('narrow'), may hold values from 0.25 to 1.75
- gate_weight: bfloat16 [7168, 18432], P('narrow', 'wide'), may hold values from -0.0625 to 0.0625
- up_weight: bfloat16 [7168, 18432], P('narrow', 'wide'), may hold values from -0.0625 to 0.0625
- down_weight: bfloat16 [18432, 7168], P('wide', 'narrow'), may hold values from -0.046875 to 0.046875
Outputs:
- residual_out: bfloat16 [128, 7168], P('wide', 'narrow')
The draws below stay inside these ranges and needn't reach their ends.
Inputs may be any that keep to these rules, and one draw needn't show every extreme that they name: `cache_lengths`: every slot has at least 256 live positions; in every draw some slot is full. `slot_rows`: each batch row is named by exactly one slot.
All inputs are finite; a program needn't handle non-finite values.
Results may differ from the reference program's by a relative error of at most 0.009.
Values may be sent and summed in bfloat16 or wider, within the bound.
A program may use at most 64 MiB of HBM per device.

```python
import math
import jax
import jax.numpy as jnp
from jax import lax

D = 7168
H = 64
HD = 128
LAT = 512
ROPE = 64
FF = 18432
LCAP = 2048
ROWS = 128


def draw_latent_cache(key, part):
    base_draw = jax.random.truncated_normal(jax.random.fold_in(key, 11), -6.0, 6.0, (ROWS, LCAP, LAT + ROPE), jnp.float32)
    return base_draw.astype(jnp.bfloat16)


def draw_query_rope(key, part):
    base_draw = jax.random.truncated_normal(jax.random.fold_in(key, 13), -6.0, 6.0, (ROWS, H, ROPE), jnp.float32)
    return base_draw.astype(jnp.bfloat16)


def draw_cache_lengths(key, part):
    drawn = jax.random.randint(jax.random.fold_in(key, 17), (ROWS,), LCAP // 8, LCAP + 1, dtype=jnp.int32)
    full_slot = jax.random.randint(jax.random.fold_in(key, 19), (), 0, ROWS, dtype=jnp.int32)
    return jnp.where(jnp.arange(ROWS, dtype=jnp.int32) == full_slot, LCAP, drawn).astype(jnp.int32)


def levels(own_key, dims, pieces, low, largest):
    def one(position, parts):
        steps = jax.random.uniform(jax.random.fold_in(jax.random.fold_in(own_key, 6), position), (parts,), jnp.float32, low / len(pieces), largest / len(pieces))
        return jnp.repeat(jnp.exp(steps), dims[position] // parts).reshape((-1,) + (1,) * (len(dims) - position - 1))

    loudness = one(*pieces[0])
    for cut in pieces[1:]:
        loudness = loudness * one(*cut)
    return loudness


def noise(own_key, shape, scale, reach, split=(), kind=jnp.bfloat16):
    gain = levels(own_key, shape, split, -0.22, 0.18) if split else 1.0
    values = jax.random.normal(own_key, shape, jnp.float32) * scale * gain
    return jnp.minimum(jnp.maximum(values, -reach), reach).astype(kind)


def setup_inputs(seed: int = 0) -> dict:
    key_list = jax.random.split(jax.random.key(seed), 14)
    return {
        "residual_in": noise(key_list[0], (ROWS, D), 0.3, 2.0, ((0, 64), (1, 4))),
        "query_nope": noise(key_list[1], (ROWS, H, HD), 1.0, 6.0, ((0, 64), (1, 4))),
        "query_rope": draw_query_rope(jax.random.fold_in(key_list[13], 71), 0),
        "absorb_key": noise(key_list[3], (H, HD, LAT), HD ** -0.5, 0.5, ((0, 4),)),
        "absorb_value": noise(key_list[4], (H, LAT, HD), LAT ** -0.5, 0.25, ((0, 4),)),
        "latent_cache": draw_latent_cache(jax.random.fold_in(key_list[13], 71), 0),
        "cache_lengths": draw_cache_lengths(jax.random.fold_in(key_list[13], 71), 0),
        "slot_rows": jax.random.permutation(key_list[7], ROWS).astype(jnp.int32),
        "out_proj": noise(key_list[8], (H * HD, D), (H * HD) ** -0.5, 0.0625, ((0, 64), (1, 4))),
        "norm_gain": jnp.clip(1.0 + 0.15 * jax.random.normal(key_list[9], (D,), jnp.float32), 0.25, 1.75).astype(jnp.bfloat16),
        "gate_weight": noise(key_list[10], (D, FF), D ** -0.5, 0.0625, ((0, 4), (1, 64))),
        "up_weight": noise(key_list[11], (D, FF), D ** -0.5, 0.0625, ((0, 4), (1, 64))),
        "down_weight": noise(key_list[12], (FF, D), FF ** -0.5, 0.046875, ((0, 64), (1, 4))),
    }


def reference(residual_in, query_nope, query_rope, absorb_key, absorb_value, latent_cache, cache_lengths, slot_rows, out_proj, norm_gain, gate_weight, up_weight, down_weight):
    query_latent = jnp.einsum('bhd,hdc->bhc', query_nope.astype(jnp.float32), absorb_key.astype(jnp.float32)).astype(jnp.bfloat16)
    queries = jnp.take(jnp.concatenate([query_latent, query_rope], axis=2), slot_rows, axis=0)
    scale = 1.0 / math.sqrt(HD + ROPE)
    positions = jnp.arange(LCAP, dtype=jnp.int32)

    def one_slot(packed):
        query_slot, cache_slot, length = packed
        scores = jnp.dot(query_slot, cache_slot.T, preferred_element_type=jnp.float32) * scale
        live = positions[None, :] < length
        scores = jnp.where(live, scores, -jnp.inf)
        highest = lax.optimization_barrier(jnp.max(scores, axis=1, keepdims=True))
        weights = jnp.where(live, jnp.exp(scores - highest), 0.0)
        probs = (weights / lax.optimization_barrier(jnp.sum(weights, axis=1, keepdims=True))).astype(jnp.bfloat16)
        context = jnp.dot(probs, cache_slot, preferred_element_type=jnp.float32)
        return context[:, :LAT].astype(jnp.bfloat16)
    context = lax.map(one_slot, (queries, latent_cache, cache_lengths))
    heads_out = jnp.einsum('shc,hcd->shd', context.astype(jnp.float32), absorb_value.astype(jnp.float32)).astype(jnp.bfloat16)
    heads_out = heads_out.reshape(ROWS, H * HD)
    slot_attn = jnp.dot(heads_out, out_proj, preferred_element_type=jnp.float32)
    attention = jnp.take(slot_attn, jnp.argsort(slot_rows), axis=0)
    middle = residual_in.astype(jnp.float32) + attention
    mean_square = lax.optimization_barrier(jnp.mean(middle * middle, axis=1, keepdims=True))
    normed = (middle * lax.rsqrt(mean_square + 1e-06) * norm_gain.astype(jnp.float32)).astype(jnp.bfloat16)
    gate = jnp.dot(normed, gate_weight, preferred_element_type=jnp.float32)
    upward = jnp.dot(normed, up_weight, preferred_element_type=jnp.float32)
    hidden = (jax.nn.silu(gate) * upward).astype(jnp.bfloat16)
    return (middle + jnp.dot(hidden, down_weight, preferred_element_type=jnp.float32)).astype(jnp.bfloat16)
```

```python
import math

import jax
import jax.numpy as jnp
from jax import lax
from jax.experimental import pallas as pl
from jax.experimental.pallas import tpu as pltpu
from jax.sharding import PartitionSpec as P

D = 7168
MESH = pl.DeviceIdType.MESH
F32 = jnp.float32
BF = jnp.bfloat16
COLS = 1792
SCALE = 1.0 / math.sqrt(192)
ANY = pl.BlockSpec(memory_space=pl.ANY)
SMEM = pl.BlockSpec(memory_space=pltpu.SMEM)
VM = pl.BlockSpec(memory_space=pltpu.VMEM)


def dot(a, b):
    return jnp.dot(a, b, preferred_element_type=F32)


def dot_nt(a, b):
    return lax.dot_general(a, b, (((1,), (1,)), ((), ())), preferred_element_type=F32)


def iota(shape, axis):
    return lax.broadcasted_iota(jnp.int32, shape, axis)


def swap_halves(tile):
    return jnp.concatenate([tile[:, 64:], tile[:, :64]], axis=1)


def kernel(
    slots, lengths, slot_vec, gain_v,
    res_h, qn_h, qr_h, ak_h, av_h, kv_h, wo_h, wg_h, wu_h, wd_h,
    out,
    res, qr, ak, av, kv, wo, wg, wu, wd, lsem,
    gq, sq, rq, a1s, a1r, a2s, a2r,
    c1b, c1r, c2f, c2b, hb, c1ss, c1rs, c2ss, c2rs,
    pm, gains, resmask,
    d0b, d0r, pown, d1b, d1r, att, asum, d2b, d2r, ss_d, rs_d,
    f1, f2, f3, ss_f, rs_f,
    g1b, g1r, hid, ss_g, rs_g,
    h0b, h0r, pown2, h1b, h1r, h2b, h2f, h2r, ss_h, rs_h,
):
    w = lax.axis_index("wide")
    x = lax.axis_index("narrow")
    y, z, c = w // 16, (w // 2) % 8, w % 2
    yc = y * 2 + c

    def wid(y_, z_, c_):
        return y_ * 16 + z_ * 2 + c_

    def rcopy(src, dst, ssem, rsem, w_, x_):
        return pltpu.make_async_remote_copy(
            src_ref=src, dst_ref=dst, send_sem=ssem, recv_sem=rsem,
            device_id=(w_, x_), device_id_type=MESH,
        )

    loads = []

    def load(src, dst):
        cp = pltpu.make_async_copy(src, dst, lsem.at[len(loads)])
        cp.start()
        loads.append(cp)
        return cp

    l_qn = load(qn_h, gq.at[yc, pl.ds(0, 2)])
    l_qr = load(qr_h, qr)
    l_ak = load(ak_h, ak)
    l_res = load(res_h, res)
    l_kv = load(kv_h, kv)
    l_av = load(av_h, av)
    l_wo = load(wo_h, wo)
    l_wg = load(wg_h, wg)
    l_wu = load(wu_h, wu)
    l_wd = load(wd_h, wd)

    bar = pltpu.get_barrier_semaphore()

    def greet(w_, x_):
        pl.semaphore_signal(bar, inc=1, device_id=(w_, x_), device_id_type=MESH)

    for k in range(1, 8):
        t = (yc + k) % 8
        greet(wid(t // 2, z, t % 2), x)
    for k in range(1, 8):
        greet(wid(y, (z + k) % 8, c), x)
    for k in range(1, 4):
        greet(w, (x + k) % 4)
    for ys in range(4):
        for cs in range(2):
            @pl.when(jnp.logical_or(x != y, jnp.logical_or(ys != y, cs != c)))
            def _():
                greet(wid(ys, z, cs), y)
    pl.semaphore_wait(bar, 25 - jnp.where(x == y, 1, 0))

    l_qr.wait()
    gq[yc, 2] = jnp.concatenate([qr[0], qr[1]], axis=1)
    l_qn.wait()
    sends = []
    cps = []
    for k in range(1, 8):
        t = (yc + k) % 8
        cp = rcopy(gq.at[yc], gq.at[yc], a1s.at[k - 1], a1r.at[k - 1], wid(t // 2, z, t % 2), x)
        cp.start()
        cps.append(cp)
    sends += cps

    sv = slot_vec[...]
    srow = (sv & 2) * 32 + (sv // 32) * 16 + ((sv // 4) & 7) * 2 + (sv & 1)
    rho = iota((128, 128), 0)
    own_first = jnp.where(rho < 64, rho + 64 * c, rho - 64 * c)
    hot = jnp.where(srow == own_first, 1.0, 0.0).astype(BF)
    sl = iota((128, 128), 0)
    sg = (sl // 32) * 32 + ((sl // 2) & 1) * 16 + ((sl // 4) & 7) * 2 + (sl & 1)
    arrange = jnp.where(sg == iota((128, 128), 1), 1.0, 0.0).astype(BF)
    pm[...] = dot(hot, arrange).astype(BF)
    l_res.wait()
    resf = res[...].astype(F32)
    spread = jnp.concatenate([resf] * 8, axis=0)
    resmask[...] = jnp.where(iota((16, COLS), 0) // 2 == z, spread, 0.0)
    gfull = gain_v[...].astype(F32)
    for j in range(7):
        gains[j] = gfull[:, 256 * j : 256 * j + 256]
    r32 = iota((32, 32), 0)
    c32 = iota((32, 32), 1)
    by_dest = jnp.where(c32 == (r32 & 1) * 16 + (r32 // 4) * 2 + ((r32 // 2) & 1), 1.0, 0.0).astype(BF)
    by_core = jnp.where(c32 == ((r32 // 2) & 7) * 4 + (r32 // 16) * 2 + (r32 & 1), 1.0, 0.0).astype(BF)

    for cp in cps:
        cp.wait_recv()

    low = iota((16, 128), 1) < 64
    for zp in range(8):
        ropes = []
        for s in range(2):
            r = slots[wid(y, zp, c) * 2 + s]
            i8 = (r // 32) * 2 + ((r // 2) & 1)
            i = r & 1
            sq[zp, s] = gq[i8, i]
            tile = gq[i8, 2].astype(F32)
            ropes.append(jnp.where(i == s, tile, swap_halves(tile)))
        sq[zp, 2] = jnp.where(low, ropes[0], ropes[1]).astype(BF)
    cps = []
    for k in range(1, 8):
        zt = (z + k) % 8
        cp = rcopy(sq.at[zt], rq.at[z], a2s.at[k - 1], a2r.at[k - 1], wid(y, zt, c), x)
        cp.start()
        cps.append(cp)
    sends += cps
    rq[z] = sq[z]
    l_ak.wait()
    l_kv.wait()
    for cp in cps:
        cp.wait_recv()

    q_parts, ropes = [], []
    for s in range(2):
        r = slots[w * 2 + s]
        zr = (r // 4) & 7
        q_parts.append(rq[zr, s])
        ropes.append(rq[zr, 2][:, 64 * s : 64 * s + 64])
    qn = jnp.concatenate(q_parts, axis=0)
    wide_q = jnp.concatenate([qn] * 16, axis=1)
    own_head = iota((32, 2048), 1) // 128 == (iota((32, 2048), 0) & 15)
    wide_q = jnp.where(own_head, wide_q, jnp.zeros_like(wide_q))
    qlat = dot(wide_q, ak[...].reshape(2048, 512)).astype(BF)
    ctxs = []
    for s in range(2):
        sc = dot_nt(qlat[16 * s : 16 * s + 16], kv[s, :, 0:512])
        sc = (sc + dot_nt(ropes[s], kv[s, :, 512:576])) * SCALE
        live = iota((16, 2048), 1) < lengths[s]
        sc = jnp.where(live, sc, -1e30)
        e = jnp.exp(sc - jnp.max(sc, axis=1, keepdims=True))
        e = jnp.where(live, e, 0.0)
        p = (e / jnp.sum(e, axis=1, keepdims=True)).astype(BF)
        ctxs.append(dot(p, kv[s, :, 0:512]).astype(BF))
    ctx = jnp.concatenate(ctxs, axis=0)
    wide_c = jnp.concatenate([ctx] * 16, axis=1)
    own_head = iota((32, 8192), 1) // 512 == (iota((32, 8192), 0) & 15)
    wide_c = jnp.where(own_head, wide_c, jnp.zeros_like(wide_c))
    l_av.wait()
    heads = dot(wide_c, av[...].reshape(8192, 128)).astype(BF)

    hp = dot(by_dest, heads)
    for zp in range(8):
        c1b[zp] = hp[4 * zp : 4 * zp + 4]
    cps = []
    for k in range(1, 8):
        zt = (z + k) % 8
        cp = rcopy(c1b.at[zt], c1r.at[z], c1ss.at[k - 1], c1rs.at[k - 1], wid(y, zt, c), x)
        cp.start()
        cps.append(cp)
    sends += cps
    c1r[z] = c1b[z]
    for cp in cps:
        cp.wait_recv()
    for zs in range(8):
        c2f[4 * zs : 4 * zs + 4] = c1r[zs]
    both = dot(by_core, c2f[...].astype(BF)).astype(BF)
    c2b[0] = both[0:16]
    c2b[1] = both[16:32]
    off_self = []
    for xt in range(4):
        for ct in range(2):
            other = jnp.logical_or(x != y, jnp.logical_or(xt != x, ct != c))
            cp = rcopy(
                c2b.at[ct], hb.at[yc], c2ss.at[xt * 2 + ct], c2rs.at[yc], wid(x, z, ct), xt
            )

            @pl.when(other)
            def _():
                cp.start()

            off_self.append((other, cp))

    @pl.when(x == y)
    def _():
        hb[yc] = c2b[c]

    l_wo.wait()
    for ys in range(4):
        for cs in range(2):
            j = ys * 2 + cs

            @pl.when(jnp.logical_or(x != y, j != yc))
            def _():
                rcopy(c2b.at[0], hb.at[j], c2ss.at[j], c2rs.at[j], wid(ys, z, cs), y).wait_recv()

    heads_all = dot(pm[...], hb[...].reshape(128, 128)).astype(BF)

    def to_core(terms, send_buf, recv_buf, own_buf, ssem, rsem):
        send_buf[...] = terms(64).astype(BF).reshape(4, 16, COLS)
        cp = rcopy(send_buf, recv_buf, ssem.at[0], rsem.at[0], wid(y, z, 1 - c), x)
        cp.start()
        own_buf[...] = terms(0).reshape(4, 16, COLS)
        cp.wait_recv()
        return cp

    def along_y(own_buf, recv_core, send_buf, recv_buf, ssem, rsem):
        for yp in range(4):
            total = own_buf[yp] + recv_core[yp].astype(F32)
            own_buf[yp] = total
            send_buf[yp] = total.astype(BF)
        cps = []
        for k in range(1, 4):
            yt = (y + k) % 4
            cp = rcopy(send_buf.at[yt], recv_buf.at[k - 1], ssem.at[k], rsem.at[k], wid(yt, z, c), x)
            cp.start()
            cps.append(cp)
        total = own_buf[y]
        for k in range(3):
            cps[k].wait_recv()
            total = total + recv_buf[k].astype(F32)
        return total, cps

    sends.append(
        to_core(lambda o: dot(heads_all[o : o + 64], wo[...]), d0b, d0r, pown, ss_d, rs_d)
    )
    total, cps = along_y(pown, d0r, d1b, d1r, ss_d, rs_d)
    sends += cps
    att[...] = total
    total = total + resmask[...]
    for j in range(7):
        piece = total[:, 256 * j : 256 * j + 256]
        asum[j] = piece
        d2b[j] = piece.astype(BF)
    guarded = []
    for k in range(1, 8):
        zt = (z + k) % 8
        cp = rcopy(
            d2b.at[lax.min(zt, 6)], d2r.at[k - 1], ss_d.at[3 + k], rs_d.at[3 + k], wid(y, zt, c), x
        )

        @pl.when(zt < 7)
        def _():
            cp.start()

        guarded.append((zt < 7, cp))

    zc = lax.min(z, 6)

    def f1_copy(k):
        zt = (z + k) % 8
        return rcopy(
            f1.at[zc], f1.at[zc], ss_f.at[k - 1], rs_f.at[k - 1], wid(y, zt, c), x
        )

    @pl.when(z < 7)
    def _():
        mid = asum[zc]
        for k in range(1, 8):
            guarded[k - 1][1].wait_recv()
            mid = mid + d2r[k - 1].astype(F32)
        f1[zc] = (mid * gains[zc]).astype(BF)
        for k in range(1, 8):
            f1_copy(k).start()

    for k in range(1, 8):
        @pl.when((z + 8 - k) % 8 < 7)
        def _():
            f1_copy(k).wait_recv()

    x16 = jnp.concatenate([f1[j] for j in range(7)], axis=1)
    f2[y, :, 0:COLS] = x16
    plain = x16.astype(F32) / gfull
    sums = jnp.sum(plain * plain, axis=1, keepdims=True)
    high = sums.astype(BF).astype(F32)
    rest = sums - high
    f2[y, :, COLS : COLS + 128] = jnp.where(iota((16, 128), 1) < 64, high, rest).astype(BF)
    ycps, ccps = [], []
    for k in range(1, 4):
        yt = (y + k) % 4
        cp = rcopy(f2.at[y], f2.at[y], ss_f.at[6 + k], rs_f.at[6 + k], wid(yt, z, c), x)
        cp.start()
        ycps.append(cp)

    def across(k):
        yb = (y + 4 - k) % 4
        cp = rcopy(f2.at[yb], f3.at[yb], ss_f.at[10 + k], rs_f.at[10 + k], wid(y, z, 1 - c), x)
        cp.start()
        ccps.append(cp)

    across(0)
    for k in range(1, 4):
        ycps[k - 1].wait_recv()
        across(k)
    sends += ycps + ccps

    l_wg.wait()
    l_wu.wait()

    def gate_up(rows, first):
        data = rows[...].reshape(64, COLS + 128)
        act = data[:, 0:COLS]
        tag = data[:, COLS:]
        gate = dot(act, wg[...]).astype(BF)
        up = dot(act, wu[...]).astype(BF)
        for b in range(2):
            g1b[first + b, :, 256:384] = tag[32 * b : 32 * b + 32]
            g1b[first + b, :, 640:768] = tag[32 * b : 32 * b + 32]
            g1b[first + b, :, 0:288] = gate[32 * b : 32 * b + 32]
            g1b[first + b, :, 384:672] = up[32 * b : 32 * b + 32]

    gate_up(f2, 0)
    for cp in ccps:
        cp.wait_recv()
    gate_up(f3, 2)
    cps = []
    for k in range(1, 4):
        xt = (x + k) % 4
        cp = rcopy(g1b.at[xt], g1r.at[k - 1], ss_g.at[k - 1], rs_g.at[k - 1], w, xt)
        cp.start()
        cps.append(cp)
    sends += cps
    total = g1b[x].astype(F32)
    for k in range(3):
        cps[k].wait_recv()
        total = total + g1r[k].astype(F32)
    square = total[:, 288:289] + total[:, 320:321]
    norm = lax.rsqrt(square / D + 1e-06)
    gate = total[:, 0:288] * norm
    up = total[:, 384:672] * norm
    hid[x] = (gate / (1.0 + jnp.exp(-gate)) * up).astype(BF)
    cps = []
    for k in range(1, 4):
        xt = (x + k) % 4
        cp = rcopy(hid.at[x], hid.at[x], ss_g.at[2 + k], rs_g.at[2 + k], w, xt)
        cp.start()
        cps.append(cp)
    sends += cps
    l_wd.wait()
    for cp in cps:
        cp.wait_recv()

    hidden = hid[...].reshape(128, 288)
    sends.append(
        to_core(lambda o: dot(hidden[o : o + 64], wd[...]), h0b, h0r, pown2, ss_h, rs_h)
    )
    total, cps = along_y(pown2, h0r, h1b, h1r, ss_h, rs_h)
    sends += cps
    total = total + att[...]
    for zp in range(8):
        piece = total[2 * zp : 2 * zp + 2]
        h2f[zp] = piece
        h2b[zp] = piece.astype(BF)
    cps = []
    for k in range(1, 8):
        zt = (z + k) % 8
        cp = rcopy(h2b.at[zt], h2r.at[k - 1], ss_h.at[3 + k], rs_h.at[3 + k], wid(y, zt, c), x)
        cp.start()
        cps.append(cp)
    sends += cps
    total = res[...].astype(F32) + h2f[z]
    for k in range(7):
        cps[k].wait_recv()
        total = total + h2r[k].astype(F32)
    out[...] = total.astype(BF)

    for cp in sends:
        cp.wait_send()
    for cond, cp in off_self + guarded:
        @pl.when(cond)
        def _():
            cp.wait_send()

    @pl.when(z < 7)
    def _():
        for k in range(1, 8):
            f1_copy(k).wait_send()


def shards(
    residual_in, query_nope, query_rope, absorb_key, absorb_value, latent_cache, cache_lengths,
    slot_rows, out_proj, norm_gain, gate_weight, up_weight, down_weight,
):
    v = pltpu.VMEM
    sem = pltpu.SemaphoreType.DMA
    scratch = [
        v((2, COLS), BF), v((2, 16, 64), BF), v((16, 128, 512), BF), v((16, 512, 128), BF),
        v((2, 2048, 576), BF), v((128, COLS), BF), v((COLS, 288), BF), v((COLS, 288), BF),
        v((288, COLS), BF), sem((10,)),
        v((8, 3, 16, 128), BF), v((8, 3, 16, 128), BF), v((8, 3, 16, 128), BF),
        sem((7,)), sem((7,)), sem((7,)), sem((7,)),
        v((8, 4, 128), F32), v((8, 4, 128), F32), v((32, 128), F32), v((2, 16, 128), BF),
        v((8, 16, 128), BF), sem((7,)), sem((7,)), sem((8,)), sem((8,)),
        v((128, 128), BF), v((7, 1, 256), F32), v((16, COLS), F32),
        v((4, 16, COLS), BF), v((4, 16, COLS), BF), v((4, 16, COLS), F32), v((4, 16, COLS), BF),
        v((3, 16, COLS), BF), v((16, COLS), F32), v((7, 16, 256), F32), v((7, 16, 256), BF),
        v((7, 16, 256), BF), sem((11,)), sem((11,)),
        v((7, 16, 256), BF), v((4, 16, COLS + 128), BF), v((4, 16, COLS + 128), BF),
        sem((14,)), sem((14,)),
        v((4, 32, 768), BF), v((3, 32, 768), BF), v((4, 32, 288), BF), sem((6,)), sem((6,)),
        v((4, 16, COLS), BF), v((4, 16, COLS), BF), v((4, 16, COLS), F32), v((4, 16, COLS), BF),
        v((3, 16, COLS), BF), v((8, 2, COLS), BF), v((8, 2, COLS), F32), v((7, 2, COLS), BF),
        sem((11,)), sem((11,)),
    ]
    return pl.pallas_call(
        kernel,
        out_shape=jax.ShapeDtypeStruct((2, COLS), BF),
        in_specs=[SMEM, SMEM, VM, VM] + [ANY] * 10,
        out_specs=VM,
        scratch_shapes=scratch,
        compiler_params=pltpu.CompilerParams(
            collective_id=0, has_side_effects=True, vmem_limit_bytes=48 * 1024 * 1024
        ),
    )(
        slot_rows, cache_lengths, slot_rows.reshape(1, 128), norm_gain.reshape(1, COLS),
        residual_in, query_nope, query_rope, absorb_key, absorb_value, latent_cache, out_proj,
        gate_weight, up_weight, down_weight,
    )


def solution(mesh):
    in_specs = (
        P("wide", "narrow"),
        P("wide", "narrow", None),
        P("wide", "narrow", None),
        P("narrow", None, None),
        P("narrow", None, None),
        P("wide", None, None),
        P("wide"),
        P(),
        P("wide", "narrow"),
        P("narrow"),
        P("narrow", "wide"),
        P("narrow", "wide"),
        P("wide", "narrow"),
    )
    out_specs = P("wide", "narrow")
    return jax.shard_map(shards, mesh=mesh, in_specs=in_specs, out_specs=out_specs, check_vma=False)
```

```python
import math

import jax
import jax.numpy as jnp
from jax import lax
from jax.experimental import pallas as pl
from jax.experimental.pallas import tpu as pltpu
from jax.sharding import PartitionSpec as P

D = 7168
MESH = pl.DeviceIdType.MESH
F32 = jnp.float32
BF = jnp.bfloat16
COLS = 1792
GROUPS = ((0, 2), (2, 4), (4, 7))
NG = len(GROUPS)
FAR_FIRST = (4, 3, 5, 2, 6, 1, 7)
SCALE = 1.0 / math.sqrt(192)
HBM = pl.BlockSpec(memory_space=pltpu.HBM)
SMEM = pl.BlockSpec(memory_space=pltpu.SMEM)
VM = pl.BlockSpec(memory_space=pltpu.VMEM)


def dot(a, b):
    return jnp.dot(a, b, preferred_element_type=F32)


def dot_nt(a, b):
    return lax.dot_general(a, b, (((1,), (1,)), ((), ())), preferred_element_type=F32)


def iota(shape, axis):
    return lax.broadcasted_iota(jnp.int32, shape, axis)


def swap_halves(tile):
    return jnp.concatenate([tile[:, 64:], tile[:, :64]], axis=1)


def kernel(
    slots, lengths, slot_vec_h, gain_h,
    res_h, qn_h, qr_h, ak_h, av_h, kv_h, wo_h, wg_h, wu_h, wd_h,
    out,
    slot_vec, gain_v, res, qr, ak, av, kv, wo, wg, wu, wd, lsem,
    gq, sq, rq, a1s, a1r, a2s, a2r,
    c1b, c1r, c2f, c2b, hb, c1ss, c1rs, c2ss, c2rs,
    pm, gains, gain_inv, resmask,
    d0b, d0r, pown, d1b, d1r, att, ss_d, rs_d, asum, d2b, d2r, ss_z, rs_z,
    f1, f2, f3, ss_f1, rs_f1, ss_f2, rs_f2, ss_f3, rs_f3,
    g1b, g1r, hid, ss_g, rs_g, ss_x, rs_x,
    h0b, h0r, pown2, h1b, h1r, ss_h, rs_h, h2b, h2f, h2r, ss_o, rs_o,
):
    w = lax.axis_index("wide")
    x = lax.axis_index("narrow")
    y, z, c = w // 16, (w // 2) % 8, w % 2
    yc = y * 2 + c

    def wid(y_, z_, c_):
        return y_ * 16 + z_ * 2 + c_

    def rcopy(src, dst, ssem, rsem, w_, x_):
        return pltpu.make_async_remote_copy(
            src_ref=src, dst_ref=dst, send_sem=ssem, recv_sem=rsem,
            device_id=(w_, x_), device_id_type=MESH,
        )

    loads, held, sends = [], [], []

    def load(src, dst):
        cp = pltpu.make_async_copy(src, dst, lsem.at[len(loads)])
        cp.start()
        loads.append(cp)
        held.append(cp)
        return cp

    def need(cp):
        held[:] = [h for h in held if h is not cp]
        cp.wait()

    def finish():
        for cp in held:
            cp.wait()
        for cond, cp in sends:
            if cond is None:
                cp.wait_send()
            else:
                @pl.when(cond)
                def _():
                    cp.wait_send()

    def send(cp, cond=None):
        sends.append((cond, cp))
        if cond is None:
            cp.start()
        else:
            @pl.when(cond)
            def _():
                cp.start()
        return cp

    bar = pltpu.get_barrier_semaphore()

    def greet(w_, x_):
        pl.semaphore_signal(bar, inc=1, device_id=(w_, x_), device_id_type=MESH)

    for k in range(1, 8):
        t = (yc + k) % 8
        greet(wid(t // 2, z, t % 2), x)
    for k in range(1, 8):
        greet(wid(y, (z + k) % 8, c), x)
    for k in range(1, 4):
        greet(w, (x + k) % 4)
    for ys in range(4):
        for cs in range(2):
            @pl.when(jnp.logical_or(x != y, jnp.logical_or(ys != y, cs != c)))
            def _():
                greet(wid(ys, z, cs), y)
    l_qn = load(qn_h, gq.at[yc, pl.ds(0, 2)])
    l_qr = load(qr_h, qr)
    l_ak = load(ak_h, ak)
    l_sv = load(slot_vec_h, slot_vec)
    l_gain = load(gain_h, gain_v)
    l_res = load(res_h, res)
    l_kv = load(kv_h, kv)
    l_av = load(av_h, av)
    l_wo = load(wo_h, wo)
    l_wg = load(wg_h, wg)
    l_wu = load(wu_h, wu)
    l_wd = load(wd_h, wd)

    pl.semaphore_wait(bar, 25 - jnp.where(x == y, 1, 0))

    need(l_qr)
    gq[yc, 2] = jnp.concatenate([qr[0], qr[1]], axis=1)
    need(l_qn)
    cps = []
    for k in (4, 5, 2, 3, 6, 7, 1):
        t = (yc + k) % 8
        cp = rcopy(gq.at[yc], gq.at[yc], a1s.at[k - 1], a1r.at[k - 1], wid(t // 2, z, t % 2), x)
        cps.append(send(cp))

    need(l_sv)
    sv = slot_vec[...]
    srow = (sv & 2) * 32 + (sv // 32) * 16 + ((sv // 4) & 7) * 2 + (sv & 1)
    rho = iota((128, 128), 0)
    own_first = jnp.where(rho < 64, rho + 64 * c, rho - 64 * c)
    hot = jnp.where(srow == own_first, 1.0, 0.0).astype(BF)
    sl = iota((128, 128), 0)
    sg = (sl // 32) * 32 + ((sl // 2) & 1) * 16 + ((sl // 4) & 7) * 2 + (sl & 1)
    arrange = jnp.where(sg == iota((128, 128), 1), 1.0, 0.0).astype(BF)
    pm[...] = dot(hot, arrange).astype(BF)
    need(l_res)
    resf = res[...].astype(F32)
    spread = jnp.concatenate([resf] * 8, axis=0)
    resmask[...] = jnp.where(iota((16, COLS), 0) // 2 == z, spread, 0.0)
    need(l_gain)
    gfull = gain_v[...].astype(F32).reshape(1, COLS)
    for j in range(7):
        gains[j] = gfull[:, 256 * j : 256 * j + 256]
    gain_inv[...] = 1.0 / gfull
    r32 = iota((32, 32), 0)
    c32 = iota((32, 32), 1)
    by_dest = jnp.where(c32 == (r32 & 1) * 16 + (r32 // 4) * 2 + ((r32 // 2) & 1), 1.0, 0.0).astype(BF)
    by_core = jnp.where(c32 == ((r32 // 2) & 7) * 4 + (r32 // 16) * 2 + (r32 & 1), 1.0, 0.0).astype(BF)

    for cp in cps:
        cp.wait_recv()

    low = iota((16, 128), 1) < 64
    for zp in range(8):
        ropes = []
        for s in range(2):
            r = slots[wid(y, zp, c) * 2 + s]
            i8 = (r // 32) * 2 + ((r // 2) & 1)
            i = r & 1
            sq[zp, s] = gq[i8, i]
            tile = gq[i8, 2].astype(F32)
            ropes.append(jnp.where(i == s, tile, swap_halves(tile)))
        sq[zp, 2] = jnp.where(low, ropes[0], ropes[1]).astype(BF)
    cps = []
    for k in FAR_FIRST:
        zt = (z + k) % 8
        cp = rcopy(sq.at[zt], rq.at[z], a2s.at[k - 1], a2r.at[k - 1], wid(y, zt, c), x)
        cps.append(send(cp))
    rq[z] = sq[z]
    need(l_ak)
    need(l_kv)
    for cp in cps:
        cp.wait_recv()

    q_parts, ropes = [], []
    for s in range(2):
        r = slots[w * 2 + s]
        zr = (r // 4) & 7
        q_parts.append(rq[zr, s])
        ropes.append(rq[zr, 2][:, 64 * s : 64 * s + 64])
    qn = jnp.concatenate(q_parts, axis=0)
    wide_q = jnp.concatenate([qn] * 16, axis=1)
    own_head = iota((32, 2048), 1) // 128 == (iota((32, 2048), 0) & 15)
    wide_q = jnp.where(own_head, wide_q, jnp.zeros_like(wide_q))
    qlat = dot(wide_q, ak[...].reshape(2048, 512)).astype(BF)
    ctxs = []
    for s in range(2):
        sc = dot(qlat[16 * s : 16 * s + 16], kv[s, 0:512])
        sc = (sc + dot(ropes[s], kv[s, 512:576])) * SCALE
        live = iota((16, 2048), 1) < lengths[s]
        sc = jnp.where(live, sc, -1e30)
        e = jnp.exp(sc - jnp.max(sc, axis=1, keepdims=True))
        e = jnp.where(live, e, 0.0)
        p = (e / jnp.sum(e, axis=1, keepdims=True)).astype(BF)
        ctxs.append(dot_nt(p, kv[s, 0:512]).astype(BF))
    ctx = jnp.concatenate(ctxs, axis=0)
    wide_c = jnp.concatenate([ctx] * 16, axis=1)
    own_head = iota((32, 8192), 1) // 512 == (iota((32, 8192), 0) & 15)
    wide_c = jnp.where(own_head, wide_c, jnp.zeros_like(wide_c))
    need(l_av)
    heads = dot(wide_c, av[...].reshape(8192, 128)).astype(BF)

    hp = dot(by_dest, heads)
    for zp in range(8):
        c1b[zp] = hp[4 * zp : 4 * zp + 4]
    cps = []
    for k in FAR_FIRST:
        zt = (z + k) % 8
        cp = rcopy(c1b.at[zt], c1r.at[z], c1ss.at[k - 1], c1rs.at[k - 1], wid(y, zt, c), x)
        cps.append(send(cp))
    c1r[z] = c1b[z]
    for cp in cps:
        cp.wait_recv()
    for zs in range(8):
        c2f[4 * zs : 4 * zs + 4] = c1r[zs]
    both = dot(by_core, c2f[...].astype(BF)).astype(BF)
    c2b[0] = both[0:16]
    c2b[1] = both[16:32]
    for xt in range(4):
        for ct in range(2):
            other = jnp.logical_or(x != y, jnp.logical_or(xt != x, ct != c))
            cp = rcopy(
                c2b.at[ct], hb.at[yc], c2ss.at[xt * 2 + ct], c2rs.at[yc], wid(x, z, ct), xt
            )

            send(cp, other)

    @pl.when(x == y)
    def _():
        hb[yc] = c2b[c]

    need(l_wo)
    for ys in range(4):
        for cs in range(2):
            j = ys * 2 + cs

            @pl.when(jnp.logical_or(x != y, j != yc))
            def _():
                rcopy(c2b.at[0], hb.at[j], c2ss.at[j], c2rs.at[j], wid(ys, z, cs), y).wait_recv()

    heads_all = dot(pm[...], hb[...].reshape(128, 128)).astype(BF)

    def to_core(terms, send_buf, recv_buf, own_buf, ssem, rsem):
        cps = []
        for g, (a, b) in enumerate(GROUPS):
            cols = slice(256 * a, 256 * b)
            send_buf[:, :, cols] = terms(64, cols).astype(BF).reshape(4, 16, -1)
            cps.append(send(rcopy(
                send_buf.at[:, :, cols], recv_buf.at[:, :, cols], ssem.at[g], rsem.at[g],
                wid(y, z, 1 - c), x,
            )))
        for a, b in GROUPS:
            cols = slice(256 * a, 256 * b)
            own_buf[:, :, cols] = terms(0, cols).reshape(4, 16, -1)
        return cps

    def along_y(core_cps, own_buf, recv_core, send_buf, recv_buf, ssem, rsem):
        cps = []
        for g, (a, b) in enumerate(GROUPS):
            cols = slice(256 * a, 256 * b)
            core_cps[g].wait_recv()
            for yp in range(4):
                total = own_buf[yp, :, cols] + recv_core[yp, :, cols].astype(F32)
                own_buf[yp, :, cols] = total
                send_buf[yp, :, cols] = total.astype(BF)
            row = []
            for k in (2, 1, 3):
                yt = (y + k) % 4
                i = NG + 3 * g + k - 1
                row.append(send(rcopy(
                    send_buf.at[yt, :, cols], recv_buf.at[k - 1, :, cols], ssem.at[i], rsem.at[i],
                    wid(yt, z, c), x,
                )))
            cps.append(row)
        return cps

    def y_total(cps, g, own_buf, recv_buf):
        cols = slice(256 * GROUPS[g][0], 256 * GROUPS[g][1])
        total = own_buf[y, :, cols]
        for cp in cps[g]:
            cp.wait_recv()
        for k in range(3):
            total = total + recv_buf[k, :, cols].astype(F32)
        return total

    cps = to_core(
        lambda o, cols: dot(heads_all[o : o + 64], wo[:, cols]), d0b, d0r, pown, ss_d, rs_d
    )
    cps = along_y(cps, pown, d0r, d1b, d1r, ss_d, rs_d)
    for g, (a, b) in enumerate(GROUPS):
        cols = slice(256 * a, 256 * b)
        total = y_total(cps, g, pown, d1r)
        att[:, cols] = total
        total = total + resmask[:, cols]
        for j in range(a, b):
            piece = total[:, 256 * (j - a) : 256 * (j - a) + 256]
            asum[j] = piece
            d2b[j] = piece.astype(BF)
            k = (j + 8 - z) % 8
            send(rcopy(d2b.at[j], d2r.at[k], ss_z.at[j], rs_z.at[k], wid(y, j, c), x), z != j)

    zc = lax.min(z, 6)

    @pl.when(z < 7)
    def _():
        mid = asum[zc]
        for k in range(1, 8):
            rcopy(d2b.at[zc], d2r.at[k], ss_z.at[zc], rs_z.at[k], wid(y, (z + k) % 8, c), x).wait_recv()
            mid = mid + d2r[k].astype(F32)
        f1[zc] = (mid * gains[zc]).astype(BF)

    for k in FAR_FIRST:
        zt = (z + k) % 8
        send(rcopy(f1.at[zc], f1.at[zc], ss_f1.at[k - 1], rs_f1.at[zc], wid(y, zt, c), x), z < 7)

    sums = jnp.zeros((16, 1), F32)
    ycps, ccps = [], []
    for g, (a, b) in enumerate(GROUPS):
        for j in range(a, b):
            @pl.when(z != j)
            def _():
                rcopy(f1.at[j], f1.at[j], ss_f1.at[0], rs_f1.at[j], wid(y, j, c), x).wait_recv()
        cols = slice(256 * a, 256 * b)
        x16 = jnp.concatenate([f1[j] for j in range(a, b)], axis=1)
        f2[y, :, cols] = x16
        plain = x16.astype(F32) * gain_inv[:, cols]
        sums = sums + jnp.sum(plain * plain, axis=1, keepdims=True)
        if g == NG - 1:
            high = sums.astype(BF).astype(F32)
            tag = jnp.where(iota((16, 128), 1) < 64, high, sums - high)
            f2[y, :, COLS : COLS + 128] = tag.astype(BF)
            cols = slice(256 * a, COLS + 128)
        row = []
        for k in (2, 1, 3):
            yt = (y + k) % 4
            i = 3 * g + k - 1
            row.append(send(rcopy(
                f2.at[y, :, cols], f2.at[y, :, cols], ss_f2.at[i], rs_f2.at[i], wid(yt, z, c), x
            )))
        ycps.append(row)
        ccps.append([send(rcopy(
            f2.at[y, :, cols], f3.at[y, :, cols], ss_f3.at[4 * g], rs_f3.at[4 * g],
            wid(y, z, 1 - c), x,
        ))])

    need(l_wg)
    need(l_wu)

    def gate_up(rows, acc, cols):
        act = rows[:, :, cols].reshape(64, -1)
        new = [dot_nt(act, wg[:, cols]), dot_nt(act, wu[:, cols])]
        return new if acc is None else [p + q for p, q in zip(acc, new)]

    def to_x(rows, acc, first):
        tag = rows[:, :, COLS:].reshape(64, 128)
        gate, up = acc[0].astype(BF), acc[1].astype(BF)
        for i in range(2):
            b = first + i
            part = slice(32 * i, 32 * i + 32)
            g1b[b, :, 256:384] = tag[part]
            g1b[b, :, 640:768] = tag[part]
            g1b[b, :, 0:288] = gate[part]
            g1b[b, :, 384:672] = up[part]
            k = (b + 4 - x) % 4
            send(rcopy(g1b.at[b], g1r.at[k], ss_g.at[b], rs_g.at[k], w, b), x != b)

    acc = None
    for g, (a, b) in enumerate(GROUPS):
        cols = slice(256 * a, 256 * b)
        full = slice(256 * a, COLS + 128) if g == NG - 1 else cols
        for n, k in enumerate((2, 1, 3)):
            ycps[g][n].wait_recv()
            yb = (y + 4 - k) % 4
            i = 4 * g + k
            ccps[g].append(send(rcopy(
                f2.at[yb, :, full], f3.at[yb, :, full], ss_f3.at[i], rs_f3.at[i],
                wid(y, z, 1 - c), x,
            )))
        acc = gate_up(f2, acc, cols)
    to_x(f2, acc, 0)
    acc = None
    for g, (a, b) in enumerate(GROUPS):
        for cp in ccps[g]:
            cp.wait_recv()
        acc = gate_up(f3, acc, slice(256 * a, 256 * b))
    to_x(f3, acc, 2)
    total = g1b[x].astype(F32)
    for k in range(1, 4):
        rcopy(g1b.at[0], g1r.at[k], ss_g.at[0], rs_g.at[k], w, (x + k) % 4).wait_recv()
        total = total + g1r[k].astype(F32)
    square = total[:, 288:289] + total[:, 320:321]
    norm = lax.rsqrt(square / D + 1e-06)
    gate = total[:, 0:288] * norm
    up = total[:, 384:672] * norm
    hid[x] = (gate / (1.0 + jnp.exp(-gate)) * up).astype(BF)
    cps = []
    for k in (2, 1, 3):
        xt = (x + k) % 4
        cp = rcopy(hid.at[x], hid.at[x], ss_x.at[k - 1], rs_x.at[k - 1], w, xt)
        cps.append(send(cp))
    need(l_wd)
    for cp in cps:
        cp.wait_recv()

    hidden = hid[...].reshape(128, 288)
    cps = to_core(
        lambda o, cols: dot(hidden[o : o + 64], wd[:, cols]), h0b, h0r, pown2, ss_h, rs_h
    )
    cps = along_y(cps, pown2, h0r, h1b, h1r, ss_h, rs_h)
    zcps = []
    for g, (a, b) in enumerate(GROUPS):
        cols = slice(256 * a, 256 * b)
        total = y_total(cps, g, pown2, h1r) + att[:, cols]
        for zp in range(8):
            piece = total[2 * zp : 2 * zp + 2]
            h2f[zp, :, cols] = piece
            h2b[zp, :, cols] = piece.astype(BF)
        row = []
        for k in FAR_FIRST:
            zt = (z + k) % 8
            i = 7 * g + k - 1
            row.append(send(rcopy(
                h2b.at[zt, :, cols], h2r.at[k - 1, :, cols], ss_o.at[i], rs_o.at[i],
                wid(y, zt, c), x,
            )))
        zcps.append(row)
    for g, (a, b) in enumerate(GROUPS):
        cols = slice(256 * a, 256 * b)
        total = res[:, cols].astype(F32) + h2f[z, :, cols]
        for cp in zcps[g]:
            cp.wait_recv()
        for k in range(7):
            total = total + h2r[k, :, cols].astype(F32)
        out[:, cols] = total.astype(BF)

    finish()


def shards(
    residual_in, query_nope, query_rope, absorb_key, absorb_value, latent_cache, cache_lengths,
    slot_rows, out_proj, norm_gain, gate_weight, up_weight, down_weight,
):
    v = pltpu.VMEM
    sem = pltpu.SemaphoreType.DMA
    scratch = [
        v((1, 128), jnp.int32), v((COLS,), BF), v((2, COLS), BF), v((2, 16, 64), BF),
        v((16, 128, 512), BF), v((16, 512, 128), BF), v((2, 576, 2048), BF), v((128, COLS), BF),
        v((288, COLS), BF), v((288, COLS), BF), v((288, COLS), BF), sem((12,)),
        v((8, 3, 16, 128), BF), v((8, 3, 16, 128), BF), v((8, 3, 16, 128), BF),
        sem((7,)), sem((7,)), sem((7,)), sem((7,)),
        v((8, 4, 128), F32), v((8, 4, 128), F32), v((32, 128), F32), v((2, 16, 128), BF),
        v((8, 16, 128), BF), sem((7,)), sem((7,)), sem((8,)), sem((8,)),
        v((128, 128), BF), v((7, 1, 256), F32), v((1, COLS), F32), v((16, COLS), F32),
        v((4, 16, COLS), BF), v((4, 16, COLS), BF), v((4, 16, COLS), F32), v((4, 16, COLS), BF),
        v((3, 16, COLS), BF), v((16, COLS), F32), sem((4 * NG,)), sem((4 * NG,)),
        v((7, 16, 256), F32), v((7, 16, 256), BF), v((8, 16, 256), BF), sem((7,)), sem((8,)),
        v((7, 16, 256), BF), v((4, 16, COLS + 128), BF), v((4, 16, COLS + 128), BF),
        sem((7,)), sem((7,)), sem((3 * NG,)), sem((3 * NG,)), sem((4 * NG,)), sem((4 * NG,)),
        v((4, 32, 768), BF), v((4, 32, 768), BF), v((4, 32, 288), BF),
        sem((4,)), sem((4,)), sem((3,)), sem((3,)),
        v((4, 16, COLS), BF), v((4, 16, COLS), BF), v((4, 16, COLS), F32), v((4, 16, COLS), BF),
        v((3, 16, COLS), BF), sem((4 * NG,)), sem((4 * NG,)),
        v((8, 2, COLS), BF), v((8, 2, COLS), F32), v((7, 2, COLS), BF),
        sem((7 * NG,)), sem((7 * NG,)),
    ]
    return pl.pallas_call(
        kernel,
        out_shape=jax.ShapeDtypeStruct((2, COLS), BF),
        in_specs=[SMEM, SMEM] + [HBM] * 12,
        out_specs=VM,
        scratch_shapes=scratch,
        compiler_params=pltpu.CompilerParams(
            collective_id=0, has_side_effects=True, vmem_limit_bytes=67043328
        ),
    )(
        slot_rows, cache_lengths, slot_rows.reshape(1, 128), norm_gain,
        residual_in, query_nope, query_rope, absorb_key, absorb_value,
        jnp.swapaxes(latent_cache, 1, 2), out_proj, gate_weight.T, up_weight.T, down_weight,
    )


def solution(mesh):
    in_specs = (
        P("wide", "narrow"),
        P("wide", "narrow", None),
        P("wide", "narrow", None),
        P("narrow", None, None),
        P("narrow", None, None),
        P("wide", None, None),
        P("wide"),
        P(),
        P("wide", "narrow"),
        P("narrow"),
        P("narrow", "wide"),
        P("narrow", "wide"),
        P("wide", "narrow"),
    )
    out_specs = P("wide", "narrow")
    return jax.shard_map(shards, mesh=mesh, in_specs=in_specs, out_specs=out_specs, check_vma=False)
```

```python
import math

import jax
import jax.numpy as jnp
from jax import lax
from jax.experimental import pallas as pl
from jax.experimental.pallas import tpu as pltpu
from jax.sharding import PartitionSpec as P

D = 7168
MESH = pl.DeviceIdType.MESH
F32 = jnp.float32
BF = jnp.bfloat16
COLS = 1792
GROUPS = ((0, 2), (2, 4), (4, 7))
NG = len(GROUPS)
FAR_FIRST = (4, 3, 5, 2, 6, 1, 7)
SCALE = 1.0 / math.sqrt(192)
HBM = pl.BlockSpec(memory_space=pltpu.HBM)
SMEM = pl.BlockSpec(memory_space=pltpu.SMEM)
VM = pl.BlockSpec(memory_space=pltpu.VMEM)


def dot(a, b):
    return jnp.dot(a, b, preferred_element_type=F32)


def dot_nt(a, b):
    return lax.dot_general(a, b, (((1,), (1,)), ((), ())), preferred_element_type=F32)


def iota(shape, axis):
    return lax.broadcasted_iota(jnp.int32, shape, axis)


def swap_halves(tile):
    return jnp.concatenate([tile[:, 64:], tile[:, :64]], axis=1)


def kernel(
    slots, lengths, slot_vec_h, gain_h,
    res_h, qn_h, qr_h, ak_h, av_h, kv_h, wo_h, wg_h, wu_h, wd_h,
    out,
    slot_vec, gain_v, res, qr, ak, av, kv, wo, wg, wu, wd, lsem,
    relay, gq, sq, rq, ss_a, rs_a, hs, hb, hf, ss_c, rs_c,
    pm, gains, gain_inv, resmask,
    d0b, d0r, pown, d1b, d1r, att, ss_d, rs_d, asum, d2b, d2r, ss_z, rs_z,
    f1, f2, f3, ss_f1, rs_f1, ss_f2, rs_f2, rs_f3,
    g1b, g1r, hid, ss_g, rs_g,
    h0b, h0r, pown2, h1b, h1r, ss_h, rs_h, h2b, h2f, h2r, ss_o, rs_o,
):
    w = lax.axis_index("wide")
    x = lax.axis_index("narrow")
    y, z, c = w // 16, (w // 2) % 8, w % 2
    yc = y * 2 + c

    def wid(y_, z_, c_):
        return y_ * 16 + z_ * 2 + c_

    def rcopy(src, dst, ssem, rsem, w_, x_):
        return pltpu.make_async_remote_copy(
            src_ref=src, dst_ref=dst, send_sem=ssem, recv_sem=rsem,
            device_id=(w_, x_), device_id_type=MESH,
        )

    loads, held = [], []

    def load(src, dst):
        cp = pltpu.make_async_copy(src, dst, lsem.at[len(loads)])
        cp.start()
        loads.append(cp)
        held.append(cp)
        return cp

    def need(cp):
        held[:] = [h for h in held if h is not cp]
        cp.wait()

    drains = []

    def finish():
        for cp in held:
            cp.wait()
        for cond, cp in drains:
            if cond is None:
                cp.wait_send()
            else:
                @pl.when(cond)
                def _():
                    cp.wait_send()

    def send(cp, cond=None):
        if cond is None:
            cp.start()
        else:
            @pl.when(cond)
            def _():
                cp.start()

    def arrivals(ref, sem):
        rcopy(ref, ref, sem, sem, w, (x + 1) % 4).wait_recv()

    def drain(ref, sem, cond=None):
        drains.append((cond, rcopy(ref, ref, sem, sem, w, (x + 1) % 4)))

    bar = pltpu.get_barrier_semaphore()

    def greet(w_, x_):
        pl.semaphore_signal(bar, inc=1, device_id=(w_, x_), device_id_type=MESH)

    for k in range(1, 8):
        t = (yc + k) % 8
        greet(wid(t // 2, z, t % 2), x)
    for k in (1, 7):
        greet(wid(y, (z + k) % 8, c), x)
    for k in range(1, 4):
        greet(w, (x + k) % 4)
    l_qn = load(qn_h, gq.at[yc, pl.ds(0, 2)])
    l_qr = load(qr_h, qr)
    l_ak = load(ak_h, ak)
    l_sv = load(slot_vec_h, slot_vec)
    l_gain = load(gain_h, gain_v)
    l_res = load(res_h, res)
    l_kv = load(kv_h, kv)
    l_av = load(av_h, av)
    l_wo = load(wo_h, wo)
    l_wg = load(wg_h, wg)
    l_wu = load(wu_h, wu)
    l_wd = load(wd_h, wd)

    pl.semaphore_wait(bar, 12)
    need(l_qr)
    gq[yc, 2] = jnp.concatenate([qr[0], qr[1]], axis=1)
    need(l_qn)
    for k in (4, 5, 2, 3, 6, 7, 1):
        t = (yc + k) % 8
        send(rcopy(gq.at[yc], gq.at[yc], ss_a.at[0], rs_a.at[0], wid(t // 2, z, t % 2), x))
    drain(gq.at[0:7], ss_a.at[0])

    def hand_on(i):
        for k in (1, 7):
            pl.semaphore_signal(
                relay.at[i], inc=1, device_id=(wid(y, (z + k) % 8, c), x), device_id_type=MESH
            )

    hand_on(0)

    need(l_sv)
    sv = slot_vec[...]
    srow = (sv & 2) * 32 + (sv // 32) * 16 + ((sv // 4) & 7) * 2 + (sv & 1)
    rho = iota((128, 128), 0)
    own_first = jnp.where(rho < 64, rho + 64 * c, rho - 64 * c)
    hot = jnp.where(srow == own_first, 1.0, 0.0).astype(BF)
    pm[...] = hot
    pl.semaphore_wait(relay.at[0], 2)
    hand_on(1)
    need(l_res)
    resf = res[...].astype(F32)
    spread = jnp.concatenate([resf] * 8, axis=0)
    resmask[...] = jnp.where(iota((16, COLS), 0) // 2 == z, spread, 0.0)
    need(l_gain)
    gfull = gain_v[...].astype(F32).reshape(1, COLS)
    for j in range(7):
        gains[j] = gfull[:, 256 * j : 256 * j + 256]
    gain_inv[...] = 1.0 / gfull
    r32 = iota((32, 32), 0)
    c32 = iota((32, 32), 1)
    by_dest = jnp.where(c32 == (r32 & 1) * 16 + (r32 // 4) * 2 + ((r32 // 2) & 1), 1.0, 0.0).astype(BF)
    pl.semaphore_wait(relay.at[1], 2)
    hand_on(2)
    pl.semaphore_wait(relay.at[2], 2)

    arrivals(gq.at[0:7], rs_a.at[0])

    low = iota((16, 128), 1) < 64
    for zp in range(8):
        ropes = []
        for s in range(2):
            r = slots[wid(y, zp, c) * 2 + s]
            i8 = (r // 32) * 2 + ((r // 2) & 1)
            i = r & 1
            sq[zp, s] = gq[i8, i]
            tile = gq[i8, 2].astype(F32)
            ropes.append(jnp.where(i == s, tile, swap_halves(tile)))
        sq[zp, 2] = jnp.where(low, ropes[0], ropes[1]).astype(BF)
    for k in FAR_FIRST:
        zt = (z + k) % 8
        send(rcopy(sq.at[zt], rq.at[z], ss_a.at[1], rs_a.at[1], wid(y, zt, c), x))
    drain(sq.at[0:7], ss_a.at[1])
    rq[z] = sq[z]
    need(l_ak)
    need(l_kv)
    arrivals(rq.at[0:7], rs_a.at[1])

    q_parts, ropes = [], []
    for s in range(2):
        r = slots[w * 2 + s]
        zr = (r // 4) & 7
        q_parts.append(rq[zr, s])
        ropes.append(rq[zr, 2][:, 64 * s : 64 * s + 64])
    qn = jnp.concatenate(q_parts, axis=0)
    wide_q = jnp.concatenate([qn] * 16, axis=1)
    own_head = iota((32, 2048), 1) // 128 == (iota((32, 2048), 0) & 15)
    wide_q = jnp.where(own_head, wide_q, jnp.zeros_like(wide_q))
    qlat = dot(wide_q, ak[...].reshape(2048, 512)).astype(BF)
    ctxs = []
    for s in range(2):
        sc = dot(qlat[16 * s : 16 * s + 16], kv[s, 0:512])
        sc = (sc + dot(ropes[s], kv[s, 512:576])) * SCALE
        live = iota((16, 2048), 1) < lengths[s]
        sc = jnp.where(live, sc, -1e30)
        e = jnp.exp(sc - jnp.max(sc, axis=1, keepdims=True))
        e = jnp.where(live, e, 0.0)
        p = (e / jnp.sum(e, axis=1, keepdims=True)).astype(BF)
        ctxs.append(dot_nt(p, kv[s, 0:512]).astype(BF))
    ctx = jnp.concatenate(ctxs, axis=0)
    wide_c = jnp.concatenate([ctx] * 16, axis=1)
    own_head = iota((32, 8192), 1) // 512 == (iota((32, 8192), 0) & 15)
    wide_c = jnp.where(own_head, wide_c, jnp.zeros_like(wide_c))
    need(l_av)
    heads = dot(wide_c, av[...].reshape(8192, 128)).astype(BF)

    hp = dot(by_dest, heads)
    for h in range(16):
        hs[h] = hp[2 * h : 2 * h + 2].astype(BF)
    home = x == y
    for kh in (8, 7, 9, 6, 10, 5, 11, 4, 12, 3, 13, 2, 14, 1, 15, 0):
        h = (2 * z + c + kh) % 16
        for kx in (2, 1, 3, 0):
            cp = rcopy(hs.at[h], hb.at[w], ss_c.at[0], rs_c.at[0], x * 16 + h, (x + kx) % 4)
            send(cp, x != y if kx == 0 and kh == 0 else None)
    drain(hb.at[0:63], ss_c.at[0], home)
    drain(hb.at[0:64], ss_c.at[0], jnp.logical_not(home))

    @pl.when(home)
    def _():
        hb[w] = hs[2 * z + c]
        arrivals(hb.at[0:63], rs_c.at[0])

    @pl.when(jnp.logical_not(home))
    def _():
        arrivals(hb.at[0:64], rs_c.at[0])

    for j in range(64):
        hf[2 * j : 2 * j + 2] = hb[j].astype(F32)
    need(l_wo)
    heads_all = dot(pm[...], hf[...].astype(BF)).astype(BF)

    def to_core(terms, send_buf, recv_buf, own_buf, sems, rsem):
        for g, (a, b) in enumerate(GROUPS):
            cols = slice(256 * a, 256 * b)
            send_buf[:, :, cols] = terms(64, cols).astype(BF).reshape(4, 16, -1)
            send(rcopy(
                send_buf.at[:, :, cols], recv_buf.at[:, :, cols], sems.at[0], rsem.at[g],
                wid(y, z, 1 - c), x,
            ))
        drain(send_buf.at[0:4], sems.at[0])
        for a, b in GROUPS:
            cols = slice(256 * a, 256 * b)
            own_buf[:, :, cols] = terms(0, cols).reshape(4, 16, -1)

    def along_y(own_buf, recv_core, send_buf, recv_buf, sems, rsem):
        for g, (a, b) in enumerate(GROUPS):
            cols = slice(256 * a, 256 * b)
            arrivals(recv_core.at[:, :, cols], rsem.at[g])
            for yp in range(4):
                total = own_buf[yp, :, cols] + recv_core[yp, :, cols].astype(F32)
                own_buf[yp, :, cols] = total
                send_buf[yp, :, cols] = total.astype(BF)
            for k in (2, 1, 3):
                yt = (y + k) % 4
                send(rcopy(
                    send_buf.at[yt, :, cols], recv_buf.at[k - 1, :, cols], sems.at[1],
                    rsem.at[NG + g], wid(yt, z, c), x,
                ))
        drain(send_buf.at[0:3], sems.at[1])

    def y_total(g, own_buf, recv_buf, rsem):
        cols = slice(256 * GROUPS[g][0], 256 * GROUPS[g][1])
        total = own_buf[y, :, cols]
        arrivals(recv_buf.at[:, :, cols], rsem.at[NG + g])
        for k in range(3):
            total = total + recv_buf[k, :, cols].astype(F32)
        return total

    to_core(lambda o, cols: dot(heads_all[o : o + 64], wo[:, cols]), d0b, d0r, pown, ss_d, rs_d)
    along_y(pown, d0r, d1b, d1r, ss_d, rs_d)
    for g, (a, b) in enumerate(GROUPS):
        cols = slice(256 * a, 256 * b)
        total = y_total(g, pown, d1r, rs_d)
        att[:, cols] = total
        total = total + resmask[:, cols]
        for j in range(a, b):
            piece = total[:, 256 * (j - a) : 256 * (j - a) + 256]
            asum[j] = piece
            d2b[j] = piece.astype(BF)
            k = (j + 8 - z) % 8
            send(rcopy(d2b.at[j], d2r.at[k], ss_z.at[0], rs_z.at[0], wid(y, j, c), x), z != j)
    drain(d2b.at[0:6], ss_z.at[0], z < 7)
    drain(d2b.at[0:7], ss_z.at[0], z == 7)

    zc = lax.min(z, 6)

    @pl.when(z < 7)
    def _():
        mid = asum[zc]
        arrivals(d2r.at[1:8], rs_z.at[0])
        for k in range(1, 8):
            mid = mid + d2r[k].astype(F32)
        f1[zc] = (mid * gains[zc]).astype(BF)

    zg = sum(jnp.where(zc >= b, 1, 0) for _, b in GROUPS[:-1])
    for k in FAR_FIRST:
        zt = (z + k) % 8
        send(rcopy(f1.at[zc], f1.at[zc], ss_f1.at[0], rs_f1.at[zg], wid(y, zt, c), x), z < 7)
    drain(f1.at[0:7], ss_f1.at[0], z < 7)

    sums = jnp.zeros((16, 1), F32)
    for g, (a, b) in enumerate(GROUPS):
        mine = jnp.logical_and(z >= a, z < b)

        @pl.when(jnp.logical_not(mine))
        def _():
            arrivals(f1.at[a:b], rs_f1.at[g])

        if b - a > 1:
            @pl.when(mine)
            def _():
                arrivals(f1.at[a : b - 1], rs_f1.at[g])

        cols = slice(256 * a, 256 * b)
        x16 = jnp.concatenate([f1[j] for j in range(a, b)], axis=1)
        f2[y, :, cols] = x16
        plain = x16.astype(F32) * gain_inv[:, cols]
        sums = sums + jnp.sum(plain * plain, axis=1, keepdims=True)
        if g == NG - 1:
            high = sums.astype(BF).astype(F32)
            tag = jnp.where(iota((16, 128), 1) < 64, high, sums - high)
            f2[y, :, COLS : COLS + 128] = tag.astype(BF)
            cols = slice(256 * a, COLS + 128)
        for k in (2, 1, 3):
            yt = (y + k) % 4
            send(rcopy(
                f2.at[y, :, cols], f2.at[y, :, cols], ss_f2.at[0], rs_f2.at[g], wid(yt, z, c), x
            ))
        send(rcopy(
            f2.at[y, :, cols], f3.at[y, :, cols], ss_f2.at[1], rs_f3.at[g], wid(y, z, 1 - c), x
        ))
    drain(f2.at[0:3], ss_f2.at[0])
    drain(f2.at[0:4], ss_f2.at[1])

    need(l_wg)
    need(l_wu)

    def gate_up(rows, acc, cols):
        act = rows[:, :, cols].reshape(64, -1)
        new = [dot_nt(act, wg[:, cols]), dot_nt(act, wu[:, cols])]
        return new if acc is None else [p + q for p, q in zip(acc, new)]

    def to_x(rows, acc, first):
        tag = rows[:, :, COLS:].reshape(64, 128)
        gate, up = acc[0].astype(BF), acc[1].astype(BF)
        for i in range(2):
            b = first + i
            part = slice(32 * i, 32 * i + 32)
            g1b[b, :, 256:384] = tag[part]
            g1b[b, :, 640:768] = tag[part]
            g1b[b, :, 0:288] = gate[part]
            g1b[b, :, 384:672] = up[part]
            k = (b + 4 - x) % 4
            send(rcopy(g1b.at[b], g1r.at[k], ss_g.at[0], rs_g.at[0], w, b), x != b)

    acc = None
    for g, (a, b) in enumerate(GROUPS):
        cols = slice(256 * a, 256 * b)
        full = slice(256 * a, COLS + 128) if g == NG - 1 else cols
        arrivals(f2.at[0:3, :, full], rs_f2.at[g])
        for k in (2, 1, 3):
            yb = (y + 4 - k) % 4
            send(rcopy(
                f2.at[yb, :, full], f3.at[yb, :, full], ss_f2.at[1], rs_f3.at[g],
                wid(y, z, 1 - c), x,
            ))
        acc = gate_up(f2, acc, cols)
    to_x(f2, acc, 0)
    acc = None
    for g, (a, b) in enumerate(GROUPS):
        full = slice(256 * a, COLS + 128) if g == NG - 1 else slice(256 * a, 256 * b)
        arrivals(f3.at[:, :, full], rs_f3.at[g])
        acc = gate_up(f3, acc, slice(256 * a, 256 * b))
    to_x(f3, acc, 2)
    drain(g1b.at[0:3], ss_g.at[0])
    total = g1b[x].astype(F32)
    arrivals(g1r.at[1:4], rs_g.at[0])
    for k in range(1, 4):
        total = total + g1r[k].astype(F32)
    square = total[:, 288:289] + total[:, 320:321]
    norm = lax.rsqrt(square / D + 1e-06)
    gate = total[:, 0:288] * norm
    up = total[:, 384:672] * norm
    hid[x] = (gate / (1.0 + jnp.exp(-gate)) * up).astype(BF)
    for k in (2, 1, 3):
        send(rcopy(hid.at[x], hid.at[x], ss_g.at[1], rs_g.at[1], w, (x + k) % 4))
    drain(hid.at[0:3], ss_g.at[1])
    need(l_wd)
    arrivals(hid.at[0:3], rs_g.at[1])

    hidden = hid[...].reshape(128, 288)
    to_core(lambda o, cols: dot(hidden[o : o + 64], wd[:, cols]), h0b, h0r, pown2, ss_h, rs_h)
    along_y(pown2, h0r, h1b, h1r, ss_h, rs_h)
    for g, (a, b) in enumerate(GROUPS):
        cols = slice(256 * a, 256 * b)
        total = y_total(g, pown2, h1r, rs_h) + att[:, cols]
        for zp in range(8):
            piece = total[2 * zp : 2 * zp + 2]
            h2f[zp, :, cols] = piece
            h2b[zp, :, cols] = piece.astype(BF)
        for k in FAR_FIRST:
            zt = (z + k) % 8
            send(rcopy(
                h2b.at[zt, :, cols], h2r.at[k - 1, :, cols], ss_o.at[0], rs_o.at[g],
                wid(y, zt, c), x,
            ))
    drain(h2b.at[0:7], ss_o.at[0])
    for g, (a, b) in enumerate(GROUPS):
        cols = slice(256 * a, 256 * b)
        total = res[:, cols].astype(F32) + h2f[z, :, cols]
        arrivals(h2r.at[:, :, cols], rs_o.at[g])
        for k in range(7):
            total = total + h2r[k, :, cols].astype(F32)
        out[:, cols] = total.astype(BF)

    finish()


def shards(
    residual_in, query_nope, query_rope, absorb_key, absorb_value, latent_cache, cache_lengths,
    slot_rows, out_proj, norm_gain, gate_weight, up_weight, down_weight,
):
    v = pltpu.VMEM
    sem = pltpu.SemaphoreType.DMA
    scratch = [
        v((1, 128), jnp.int32), v((COLS,), BF), v((2, COLS), BF), v((2, 16, 64), BF),
        v((16, 128, 512), BF), v((16, 512, 128), BF), v((2, 576, 2048), BF), v((128, COLS), BF),
        v((288, COLS), BF), v((288, COLS), BF), v((288, COLS), BF), sem((12,)),
        pltpu.SemaphoreType.REGULAR((3,)),
        v((8, 3, 16, 128), BF), v((8, 3, 16, 128), BF), v((8, 3, 16, 128), BF), sem((2,)), sem((2,)),
        v((16, 2, 128), BF), v((64, 2, 128), BF), v((128, 128), F32), sem((1,)), sem((1,)),
        v((128, 128), BF), v((7, 1, 256), F32), v((1, COLS), F32), v((16, COLS), F32),
        v((4, 16, COLS), BF), v((4, 16, COLS), BF), v((4, 16, COLS), F32), v((4, 16, COLS), BF),
        v((3, 16, COLS), BF), v((16, COLS), F32), sem((2,)), sem((2 * NG,)),
        v((7, 16, 256), F32), v((7, 16, 256), BF), v((8, 16, 256), BF), sem((1,)), sem((1,)),
        v((7, 16, 256), BF), v((4, 16, COLS + 128), BF), v((4, 16, COLS + 128), BF),
        sem((1,)), sem((NG,)), sem((2,)), sem((NG,)), sem((NG,)),
        v((4, 32, 768), BF), v((4, 32, 768), BF), v((4, 32, 288), BF),
        sem((2,)), sem((2,)),
        v((4, 16, COLS), BF), v((4, 16, COLS), BF), v((4, 16, COLS), F32), v((4, 16, COLS), BF),
        v((3, 16, COLS), BF), sem((2,)), sem((2 * NG,)),
        v((8, 2, COLS), BF), v((8, 2, COLS), F32), v((7, 2, COLS), BF),
        sem((1,)), sem((NG,)),
    ]
    return pl.pallas_call(
        kernel,
        out_shape=jax.ShapeDtypeStruct((2, COLS), BF),
        in_specs=[SMEM, SMEM] + [HBM] * 12,
        out_specs=VM,
        scratch_shapes=scratch,
        compiler_params=pltpu.CompilerParams(
            collective_id=0, has_side_effects=True, vmem_limit_bytes=67043328
        ),
    )(
        slot_rows, cache_lengths, slot_rows.reshape(1, 128), norm_gain,
        residual_in, query_nope, query_rope, absorb_key, absorb_value,
        jnp.swapaxes(latent_cache, 1, 2), out_proj, gate_weight.T, up_weight.T, down_weight,
    )


def solution(mesh):
    in_specs = (
        P("wide", "narrow"),
        P("wide", "narrow", None),
        P("wide", "narrow", None),
        P("narrow", None, None),
        P("narrow", None, None),
        P("wide", None, None),
        P("wide"),
        P(),
        P("wide", "narrow"),
        P("narrow"),
        P("narrow", "wide"),
        P("narrow", "wide"),
        P("wide", "narrow"),
    )
    out_specs = P("wide", "narrow")
    return jax.shard_map(shards, mesh=mesh, in_specs=in_specs, out_specs=out_specs, check_vma=False)
```

```python
import math

import jax
import jax.numpy as jnp
from jax import lax
from jax.experimental import pallas as pl
from jax.experimental.pallas import tpu as pltpu
from jax.sharding import PartitionSpec as P

D = 7168
MESH = pl.DeviceIdType.MESH
F32 = jnp.float32
BF = jnp.bfloat16
COLS = 1792
HALF = COLS // 2
GROUPS = ((0, 1), (1, 3), (3, 5), (5, 7))
NG = len(GROUPS)
FAR_FIRST = (4, 3, 5, 2, 6, 1, 7)
SCALE = 1.0 / math.sqrt(192)
HBM = pl.BlockSpec(memory_space=pltpu.HBM)
SMEM = pl.BlockSpec(memory_space=pltpu.SMEM)
VM = pl.BlockSpec(memory_space=pltpu.VMEM)


def dot(a, b):
    return jnp.dot(a, b, preferred_element_type=F32)


def dot_nt(a, b):
    return lax.dot_general(a, b, (((1,), (1,)), ((), ())), preferred_element_type=F32)


def iota(shape, axis):
    return lax.broadcasted_iota(jnp.int32, shape, axis)


def swap_halves(tile):
    return jnp.concatenate([tile[:, 64:], tile[:, :64]], axis=1)


def kernel(
    slots, lengths, slot_vec_h, gain_h,
    res_h, qn_h, qr_h, ak_h, av_h, kv_h, wo_h, wg_h, wu_h, wd_h,
    out,
    slot_vec, gain_v, res, qr, ak, av, kv, wo, wga, wgb, wua, wub, wd, lsem,
    relay, gq, sq, rq, ss_a, rs_a, hs, hb, hf, ss_c, rs_c,
    pm, gains, inv_own, inv_other, resx, resmask, ss_w, rs_w,
    pown, d1b, d1r, ss_d, rs_d, asum, d2b, d2r, ss_z, rs_z,
    f1, f2, f3, mrow, ss_f1, rs_f1, ss_f2, rs_f2, rs_f3,
    g1b, g1r, hid, ss_g, rs_g,
    h0b, h0r, pown2, h1b, h1r, ss_h, rs_h, h2b, h2f, h2r, ss_o, rs_o,
):
    w = lax.axis_index("wide")
    x = lax.axis_index("narrow")
    y, z, c = w // 16, (w // 2) % 8, w % 2
    yc = y * 2 + c
    own_cols = pl.ds(pl.multiple_of(c * HALF, 128), HALF)
    other_cols = pl.ds(pl.multiple_of((1 - c) * HALF, 128), HALF)

    def wid(y_, z_, c_):
        return y_ * 16 + z_ * 2 + c_

    def rcopy(src, dst, ssem, rsem, w_, x_):
        return pltpu.make_async_remote_copy(
            src_ref=src, dst_ref=dst, send_sem=ssem, recv_sem=rsem,
            device_id=(w_, x_), device_id_type=MESH,
        )

    loads, held = [], []

    def load(src, dst):
        cp = pltpu.make_async_copy(src, dst, lsem.at[len(loads)])
        cp.start()
        loads.append(cp)
        held.append(cp)
        return cp

    def need(cp):
        held[:] = [h for h in held if h is not cp]
        cp.wait()

    drains = []

    def finish():
        for cp in held:
            cp.wait()
        for cond, cp in drains:
            if cond is None:
                cp.wait_send()
            else:
                @pl.when(cond)
                def _():
                    cp.wait_send()

    def send(cp, cond=None):
        if cond is None:
            cp.start()
        else:
            @pl.when(cond)
            def _():
                cp.start()

    def arrivals(ref, sem):
        rcopy(ref, ref, sem, sem, w, (x + 1) % 4).wait_recv()

    def drain(ref, sem, cond=None):
        drains.append((cond, rcopy(ref, ref, sem, sem, w, (x + 1) % 4)))

    bar = pltpu.get_barrier_semaphore()

    def greet(w_, x_):
        pl.semaphore_signal(bar, inc=1, device_id=(w_, x_), device_id_type=MESH)

    for k in range(1, 8):
        t = (yc + k) % 8
        greet(wid(t // 2, z, t % 2), x)
    for k in (1, 7):
        greet(wid(y, (z + k) % 8, c), x)
    for k in range(1, 4):
        greet(w, (x + k) % 4)
    l_qn = load(qn_h, gq.at[yc, pl.ds(0, 2)])
    l_qr = load(qr_h, qr)
    l_ak = load(ak_h, ak)
    l_sv = load(slot_vec_h, slot_vec)
    l_gain = load(gain_h, gain_v)
    l_res = load(res_h, res)
    l_kv = load(kv_h, kv)
    l_av = load(av_h, av)
    l_wo = load(wo_h.at[:, own_cols], wo.at[0:128])
    l_wga = load(wg_h.at[:, own_cols], wga)
    l_wua = load(wu_h.at[:, own_cols], wua)
    l_wgb = load(wg_h.at[:, other_cols], wgb)
    l_wub = load(wu_h.at[:, other_cols], wub)
    l_wd = load(wd_h, wd)

    pl.semaphore_wait(bar, 12)
    need(l_qr)
    gq[yc, 2] = jnp.concatenate([qr[0], qr[1]], axis=1)
    need(l_qn)
    for k in (4, 5, 2, 3, 6, 7, 1):
        t = (yc + k) % 8
        send(rcopy(gq.at[yc], gq.at[yc], ss_a.at[0], rs_a.at[0], wid(t // 2, z, t % 2), x))
    drain(gq.at[0:7], ss_a.at[0])
    partner = wid(y, z, 1 - c)
    send(rcopy(res_h.at[:, other_cols], resx, ss_w.at[0], rs_w.at[0], partner, x))
    send(rcopy(wo_h.at[:, other_cols], wo.at[128:256], ss_w.at[1], rs_w.at[1], partner, x))
    drain(resx, ss_w.at[0])
    drain(wo.at[128:256], ss_w.at[1])

    def hand_on(i):
        for k in (1, 7):
            pl.semaphore_signal(
                relay.at[i], inc=1, device_id=(wid(y, (z + k) % 8, c), x), device_id_type=MESH
            )

    hand_on(0)

    need(l_sv)
    sv = slot_vec[...]
    srow = (sv // 32) * 32 + ((sv // 2) & 1) * 16 + ((sv // 4) & 7) * 2 + (sv & 1)
    pm[...] = jnp.where(srow == iota((128, 128), 0), 1.0, 0.0).astype(BF)
    pl.semaphore_wait(relay.at[0], 2)
    hand_on(1)
    need(l_res)
    need(l_gain)
    gfull = gain_v[...].astype(F32).reshape(1, COLS)
    left, right = gfull[:, :HALF], gfull[:, HALF:]
    gain_own = jnp.where(c == 0, left, right)
    inv_own[...] = 1.0 / gain_own
    inv_other[...] = 1.0 / jnp.where(c == 0, right, left)
    for j in range(7):
        gains[j] = gain_own[:, 128 * j : 128 * j + 128]
    r32 = iota((32, 32), 0)
    c32 = iota((32, 32), 1)
    by_dest = jnp.where(c32 == (r32 & 1) * 16 + (r32 // 4) * 2 + ((r32 // 2) & 1), 1.0, 0.0).astype(BF)
    pl.semaphore_wait(relay.at[1], 2)
    hand_on(2)
    pl.semaphore_wait(relay.at[2], 2)

    arrivals(gq.at[0:7], rs_a.at[0])

    low = iota((16, 128), 1) < 64
    for zp in range(8):
        ropes = []
        for s in range(2):
            r = slots[wid(y, zp, c) * 2 + s]
            i8 = (r // 32) * 2 + ((r // 2) & 1)
            i = r & 1
            sq[zp, s] = gq[i8, i]
            tile = gq[i8, 2].astype(F32)
            ropes.append(jnp.where(i == s, tile, swap_halves(tile)))
        sq[zp, 2] = jnp.where(low, ropes[0], ropes[1]).astype(BF)
    for k in FAR_FIRST:
        zt = (z + k) % 8
        send(rcopy(sq.at[zt], rq.at[z], ss_a.at[1], rs_a.at[1], wid(y, zt, c), x))
    drain(sq.at[0:7], ss_a.at[1])
    rq[z] = sq[z]
    arrivals(resx, rs_w.at[0])
    mine = jnp.where(c == 0, res[:, :HALF], res[:, HALF:]).astype(F32)
    theirs = resx[...].astype(F32)
    top = jnp.where(c == 0, mine, theirs)
    low2 = jnp.where(c == 0, theirs, mine)
    spread = jnp.concatenate([top] * 8 + [low2] * 8, axis=0)
    resmask[...] = jnp.where((iota((32, HALF), 0) // 2) % 8 == z, spread, 0.0)
    need(l_ak)
    need(l_kv)
    arrivals(rq.at[0:7], rs_a.at[1])

    q_parts, ropes = [], []
    for s in range(2):
        r = slots[w * 2 + s]
        zr = (r // 4) & 7
        q_parts.append(rq[zr, s])
        ropes.append(rq[zr, 2][:, 64 * s : 64 * s + 64])
    qn = jnp.concatenate(q_parts, axis=0)
    wide_q = jnp.concatenate([qn] * 16, axis=1)
    own_head = iota((32, 2048), 1) // 128 == (iota((32, 2048), 0) & 15)
    wide_q = jnp.where(own_head, wide_q, jnp.zeros_like(wide_q))
    qlat = dot(wide_q, ak[...].reshape(2048, 512)).astype(BF)
    ctxs = []
    for s in range(2):
        sc = dot(qlat[16 * s : 16 * s + 16], kv[s, 0:512])
        sc = (sc + dot(ropes[s], kv[s, 512:576])) * SCALE
        live = iota((16, 2048), 1) < lengths[s]
        sc = jnp.where(live, sc, -1e30)
        e = jnp.exp(sc - jnp.max(sc, axis=1, keepdims=True))
        e = jnp.where(live, e, 0.0)
        p = (e / jnp.sum(e, axis=1, keepdims=True)).astype(BF)
        ctxs.append(dot_nt(p, kv[s, 0:512]).astype(BF))
    ctx = jnp.concatenate(ctxs, axis=0)
    wide_c = jnp.concatenate([ctx] * 16, axis=1)
    own_head = iota((32, 8192), 1) // 512 == (iota((32, 8192), 0) & 15)
    wide_c = jnp.where(own_head, wide_c, jnp.zeros_like(wide_c))
    need(l_av)
    heads = dot(wide_c, av[...].reshape(8192, 128)).astype(BF)

    hp = dot(by_dest, heads)
    for zt in range(8):
        hs[zt] = hp[4 * zt : 4 * zt + 4].astype(BF)
    home = x == y
    for kz in FAR_FIRST + (0,):
        zt = (z + kz) % 8
        for kx in (2, 1, 3, 0):
            for kc in (1, 0):
                cp = rcopy(
                    hs.at[zt], hb.at[w], ss_c.at[0], rs_c.at[0],
                    wid(x, zt, (c + kc) % 2), (x + kx) % 4,
                )
                send(cp, x != y if kx == 0 and kz == 0 and kc == 0 else None)
    drain(hb.at[0:63], ss_c.at[0], home)
    drain(hb.at[0:64], ss_c.at[0], jnp.logical_not(home))

    @pl.when(home)
    def _():
        hb[w] = hs[z]
        arrivals(hb.at[0:63], rs_c.at[0])

    @pl.when(jnp.logical_not(home))
    def _():
        arrivals(hb.at[0:64], rs_c.at[0])

    for j in range(64):
        two = hb[j].astype(F32)
        hf[0, 2 * j : 2 * j + 2] = two[0:2]
        hf[1, 2 * j : 2 * j + 2] = two[2:4]
    need(l_wo)
    arrivals(wo.at[128:256], rs_w.at[1])
    both = jnp.concatenate([hf[c], hf[1 - c]], axis=1).astype(BF)
    heads_all = dot(pm[...], both).astype(BF)

    for g, (a, b) in enumerate(GROUPS):
        cols = slice(128 * a, 128 * b)
        part = dot(heads_all, wo[:, cols]).reshape(4, 32, -1)
        pown[:, :, cols] = part
        d1b[:, :, cols] = part.astype(BF)
        for k in (2, 1, 3):
            yt = (y + k) % 4
            send(rcopy(
                d1b.at[yt, :, cols], d1r.at[k - 1, :, cols], ss_d.at[0], rs_d.at[g],
                wid(yt, z, c), x,
            ))
    drain(d1b.at[0:3], ss_d.at[0])
    for g, (a, b) in enumerate(GROUPS):
        cols = slice(128 * a, 128 * b)
        total = pown[y, :, cols] + resmask[:, cols]
        arrivals(d1r.at[:, :, cols], rs_d.at[g])
        for k in range(3):
            total = total + d1r[k, :, cols].astype(F32)
        for j in range(a, b):
            piece = total[:, 128 * (j - a) : 128 * (j - a) + 128]
            asum[j] = piece
            d2b[j] = piece.astype(BF)
            k = (j + 8 - z) % 8
            send(rcopy(d2b.at[j], d2r.at[k], ss_z.at[0], rs_z.at[0], wid(y, j, c), x), z != j)
    drain(d2b.at[0:6], ss_z.at[0], z < 7)
    drain(d2b.at[0:7], ss_z.at[0], z == 7)

    zc = lax.min(z, 6)

    @pl.when(z < 7)
    def _():
        mid = asum[zc]
        arrivals(d2r.at[1:8], rs_z.at[0])
        for k in range(1, 8):
            mid = mid + d2r[k].astype(F32)
        f1[zc] = (mid * gains[zc]).astype(BF)

    zg = sum(jnp.where(zc >= b, 1, 0) for _, b in GROUPS[:-1])
    for k in FAR_FIRST:
        zt = (z + k) % 8
        send(rcopy(f1.at[zc], f1.at[zc], ss_f1.at[0], rs_f1.at[zg], wid(y, zt, c), x), z < 7)
    drain(f1.at[0:7], ss_f1.at[0], z < 7)

    sums = jnp.zeros((32, 1), F32)
    for g, (a, b) in enumerate(GROUPS):
        mine = jnp.logical_and(z >= a, z < b)

        @pl.when(jnp.logical_not(mine))
        def _():
            arrivals(f1.at[a:b], rs_f1.at[g])

        if b - a > 1:
            @pl.when(mine)
            def _():
                arrivals(f1.at[a : b - 1], rs_f1.at[g])

        cols = slice(128 * a, 128 * b)
        x16 = jnp.concatenate([f1[j] for j in range(a, b)], axis=1)
        f2[y, :, cols] = x16
        plain = x16.astype(F32) * inv_own[:, cols]
        sums = sums + jnp.sum(plain * plain, axis=1, keepdims=True)
        if g == NG - 1:
            high = sums.astype(BF).astype(F32)
            tag = jnp.where(iota((32, 128), 1) < 64, high, sums - high)
            f2[y, :, HALF : HALF + 128] = tag.astype(BF)
            cols = slice(128 * a, HALF + 128)
        for k in (2, 1, 3):
            yt = (y + k) % 4
            send(rcopy(
                f2.at[y, :, cols], f2.at[y, :, cols], ss_f2.at[0], rs_f2.at[g], wid(yt, z, c), x
            ))
        send(rcopy(
            f2.at[y, :, cols], f3.at[y, :, cols], ss_f2.at[1], rs_f3.at[g], wid(y, z, 1 - c), x
        ))
    drain(f2.at[0:3], ss_f2.at[0])
    drain(f2.at[0:4], ss_f2.at[1])

    need(l_wga)
    need(l_wua)

    def gate_up(acc, rows, w_gate, w_up, g):
        cols = slice(128 * GROUPS[g][0], 128 * GROUPS[g][1])
        act = rows[:, :, cols].reshape(128, -1)
        new = [dot_nt(act, w_gate[:, cols]), dot_nt(act, w_up[:, cols])]
        return new if acc is None else [p + q for p, q in zip(acc, new)]

    def span(g):
        a, b = GROUPS[g]
        return slice(128 * a, HALF + 128 if g == NG - 1 else 128 * b)

    acc = None
    for g in range(NG):
        arrivals(f2.at[0:3, :, span(g)], rs_f2.at[g])
        for k in (2, 1, 3):
            yb = (y + 4 - k) % 4
            send(rcopy(
                f2.at[yb, :, span(g)], f3.at[yb, :, span(g)], ss_f2.at[1], rs_f3.at[g],
                wid(y, z, 1 - c), x,
            ))
        acc = gate_up(acc, f2, wga, wua, g)
    need(l_wgb)
    need(l_wub)
    for g in range(NG):
        arrivals(f3.at[:, :, span(g)], rs_f3.at[g])
        acc = gate_up(acc, f3, wgb, wub, g)
    tags = f2[:, :, HALF:].reshape(128, 128).astype(F32) + f3[:, :, HALF:].reshape(128, 128).astype(F32)
    sums = tags[:, 0:1] + tags[:, 64:65]
    high = sums.astype(BF).astype(F32)
    tag = jnp.where(iota((128, 128), 1) < 64, high, sums - high).astype(BF)
    gate, up = acc[0].astype(BF), acc[1].astype(BF)
    for b in range(4):
        part = slice(32 * b, 32 * b + 32)
        g1b[b, :, 256:384] = tag[part]
        g1b[b, :, 640:768] = tag[part]
        g1b[b, :, 0:288] = gate[part]
        g1b[b, :, 384:672] = up[part]
    for k in (2, 1, 3):
        xt = (x + k) % 4
        send(rcopy(g1b.at[xt], g1r.at[k], ss_g.at[0], rs_g.at[0], w, xt))

    pick = jnp.where(iota((16, 32), 1) == c * 16 + z * 2 + iota((16, 32), 0), 1.0, 0.0).astype(BF)
    here = dot(pick, f2[y, :, 0:HALF])[0:2] * inv_own[...]
    there = dot(pick, f3[y, :, 0:HALF])[0:2] * inv_other[...]
    mrow[:, 0:HALF] = jnp.where(c == 0, here, there)
    mrow[:, HALF:COLS] = jnp.where(c == 0, there, here)
    drain(g1b.at[0:3], ss_g.at[0])
    total = g1b[x].astype(F32)
    arrivals(g1r.at[1:4], rs_g.at[0])
    for k in range(1, 4):
        total = total + g1r[k].astype(F32)
    square = total[:, 288:289] + total[:, 320:321]
    norm = lax.rsqrt(square / D + 1e-06)
    gate = total[:, 0:288] * norm
    up = total[:, 384:672] * norm
    hid[x] = (gate / (1.0 + jnp.exp(-gate)) * up).astype(BF)
    for k in (2, 1, 3):
        send(rcopy(hid.at[x], hid.at[x], ss_g.at[1], rs_g.at[1], w, (x + k) % 4))
    drain(hid.at[0:3], ss_g.at[1])
    need(l_wd)
    arrivals(hid.at[0:3], rs_g.at[1])

    def to_core(terms, send_buf, recv_buf, own_buf, sems, rsem):
        for g, (a, b) in enumerate(GROUPS):
            cols = slice(256 * a, 256 * b)
            send_buf[:, :, cols] = terms(1, cols).astype(BF).reshape(4, 16, -1)
            send(rcopy(
                send_buf.at[:, :, cols], recv_buf.at[:, :, cols], sems.at[0], rsem.at[g],
                wid(y, z, 1 - c), x,
            ))
        drain(send_buf.at[0:4], sems.at[0])
        for a, b in GROUPS:
            cols = slice(256 * a, 256 * b)
            own_buf[:, :, cols] = terms(0, cols).reshape(4, 16, -1)

    def along_y(own_buf, recv_core, send_buf, recv_buf, sems, rsem):
        for g, (a, b) in enumerate(GROUPS):
            cols = slice(256 * a, 256 * b)
            arrivals(recv_core.at[:, :, cols], rsem.at[g])
            for yp in range(4):
                total = own_buf[yp, :, cols] + recv_core[yp, :, cols].astype(F32)
                own_buf[yp, :, cols] = total
                send_buf[yp, :, cols] = total.astype(BF)
            for k in (2, 1, 3):
                yt = (y + k) % 4
                send(rcopy(
                    send_buf.at[yt, :, cols], recv_buf.at[k - 1, :, cols], sems.at[1],
                    rsem.at[NG + g], wid(yt, z, c), x,
                ))
        drain(send_buf.at[0:3], sems.at[1])

    def y_total(g, own_buf, recv_buf, rsem):
        cols = slice(256 * GROUPS[g][0], 256 * GROUPS[g][1])
        total = own_buf[y, :, cols]
        arrivals(recv_buf.at[:, :, cols], rsem.at[NG + g])
        for k in range(3):
            total = total + recv_buf[k, :, cols].astype(F32)
        return total

    def hidden_of(core):
        return hid[:, pl.ds(pl.multiple_of(core * 16, 16), 16), :].reshape(64, 288)

    hidden = [hidden_of(c), hidden_of(1 - c)]
    to_core(lambda n, cols: dot(hidden[n], wd[:, cols]), h0b, h0r, pown2, ss_h, rs_h)
    along_y(pown2, h0r, h1b, h1r, ss_h, rs_h)
    for g, (a, b) in enumerate(GROUPS):
        cols = slice(256 * a, 256 * b)
        total = y_total(g, pown2, h1r, rs_h)
        for zp in range(8):
            piece = total[2 * zp : 2 * zp + 2]
            h2f[zp, :, cols] = piece
            h2b[zp, :, cols] = piece.astype(BF)
        for k in FAR_FIRST:
            zt = (z + k) % 8
            send(rcopy(
                h2b.at[zt, :, cols], h2r.at[k - 1, :, cols], ss_o.at[0], rs_o.at[g],
                wid(y, zt, c), x,
            ))
    drain(h2b.at[0:7], ss_o.at[0])
    for g, (a, b) in enumerate(GROUPS):
        cols = slice(256 * a, 256 * b)
        total = mrow[:, cols] + h2f[z, :, cols]
        arrivals(h2r.at[:, :, cols], rs_o.at[g])
        for k in range(7):
            total = total + h2r[k, :, cols].astype(F32)
        out[:, cols] = total.astype(BF)

    finish()


def shards(
    residual_in, query_nope, query_rope, absorb_key, absorb_value, latent_cache, cache_lengths,
    slot_rows, out_proj, norm_gain, gate_weight, up_weight, down_weight,
):
    v = pltpu.VMEM
    sem = pltpu.SemaphoreType.DMA
    scratch = [
        v((1, 128), jnp.int32), v((COLS,), BF), v((2, COLS), BF), v((2, 16, 64), BF),
        v((16, 128, 512), BF), v((16, 512, 128), BF), v((2, 576, 2048), BF), v((256, HALF), BF),
        v((288, HALF), BF), v((288, HALF), BF), v((288, HALF), BF), v((288, HALF), BF),
        v((288, COLS), BF), sem((14,)),
        pltpu.SemaphoreType.REGULAR((3,)),
        v((8, 3, 16, 128), BF), v((8, 3, 16, 128), BF), v((8, 3, 16, 128), BF), sem((2,)), sem((2,)),
        v((8, 4, 128), BF), v((64, 4, 128), BF), v((2, 128, 128), F32), sem((1,)), sem((1,)),
        v((128, 128), BF), v((7, 1, 128), F32), v((1, HALF), F32), v((1, HALF), F32),
        v((2, HALF), BF), v((32, HALF), F32), sem((2,)), sem((2,)),
        v((4, 32, HALF), F32), v((4, 32, HALF), BF), v((3, 32, HALF), BF), sem((1,)), sem((NG,)),
        v((7, 32, 128), F32), v((7, 32, 128), BF), v((8, 32, 128), BF), sem((1,)), sem((1,)),
        v((7, 32, 128), BF), v((4, 32, HALF + 128), BF), v((4, 32, HALF + 128), BF),
        v((2, COLS), F32), sem((1,)), sem((NG,)), sem((2,)), sem((NG,)), sem((NG,)),
        v((4, 32, 768), BF), v((4, 32, 768), BF), v((4, 32, 288), BF), sem((2,)), sem((2,)),
        v((4, 16, COLS), BF), v((4, 16, COLS), BF), v((4, 16, COLS), F32), v((4, 16, COLS), BF),
        v((3, 16, COLS), BF), sem((2,)), sem((2 * NG,)),
        v((8, 2, COLS), BF), v((8, 2, COLS), F32), v((7, 2, COLS), BF), sem((1,)), sem((NG,)),
    ]
    return pl.pallas_call(
        kernel,
        out_shape=jax.ShapeDtypeStruct((2, COLS), BF),
        in_specs=[SMEM, SMEM] + [HBM] * 12,
        out_specs=VM,
        scratch_shapes=scratch,
        compiler_params=pltpu.CompilerParams(
            collective_id=0, has_side_effects=True, vmem_limit_bytes=67043328
        ),
    )(
        slot_rows, cache_lengths, slot_rows.reshape(1, 128), norm_gain,
        residual_in, query_nope, query_rope, absorb_key, absorb_value,
        jnp.swapaxes(latent_cache, 1, 2), out_proj, gate_weight.T, up_weight.T, down_weight,
    )


def solution(mesh):
    in_specs = (
        P("wide", "narrow"),
        P("wide", "narrow", None),
        P("wide", "narrow", None),
        P("narrow", None, None),
        P("narrow", None, None),
        P("wide", None, None),
        P("wide"),
        P(),
        P("wide", "narrow"),
        P("narrow"),
        P("narrow", "wide"),
        P("narrow", "wide"),
        P("wide", "narrow"),
    )
    out_specs = P("wide", "narrow")
    return jax.shard_map(shards, mesh=mesh, in_specs=in_specs, out_specs=out_specs, check_vma=False)
```

```python
import math

import jax
import jax.numpy as jnp
from jax import lax
from jax.experimental import pallas as pl
from jax.experimental.pallas import tpu as pltpu
from jax.sharding import PartitionSpec as P

D = 7168
MESH = pl.DeviceIdType.MESH
F32 = jnp.float32
BF = jnp.bfloat16
COLS = 1792
HALF = COLS // 2
GROUPS = ((0, 2), (2, 4), (4, 6), (6, 7))
NG = len(GROUPS)
LAST = ((0, 1), (2, 3))
FAR_FIRST = (4, 3, 5, 2, 6, 1, 7)
SCALE = 1.0 / math.sqrt(192)
HBM = pl.BlockSpec(memory_space=pltpu.HBM)
VM = pl.BlockSpec(memory_space=pltpu.VMEM)


def dot(a, b):
    return jnp.dot(a, b, preferred_element_type=F32)


def dot_nt(a, b):
    return lax.dot_general(a, b, (((1,), (1,)), ((), ())), preferred_element_type=F32)


def iota(shape, axis):
    return lax.broadcasted_iota(jnp.int32, shape, axis)


def swap_halves(tile):
    return jnp.concatenate([tile[:, 64:], tile[:, :64]], axis=1)


def kernel(
    slots_h, lengths_h, slot_vec_h, gain_h,
    res_h, qn_h, qr_h, ak_h, av_h, kv_h, wo_h, wg_h, wu_h, wd_h,
    out,
    slots, lengths, slot_vec, gain_v, res, qr, ak, av, kv, wo, wga, wgb, wua, wub, wd, lsem,
    relay, gq, sq, rq, ss_a, rs_a, hs, hb, hf, ss_c, rs_c,
    pm, gains, inv_own, inv_other, resx, resmask, ss_w, rs_w,
    pown, d1b, d1r, ss_d, rs_d, asum, d2b, d2r, ss_z, rs_z,
    f1, f2, f3, mrow, ss_f1, rs_f1, ss_f2, rs_f2, rs_f3,
    g1b, g1r, hid, ss_g, rs_g,
    pown2, h1b, h1r, ss_h, rs_h, h2b, h2f, h2r, ss_o, rs_o,
):
    w = lax.axis_index("wide")
    x = lax.axis_index("narrow")
    y, z, c = w // 16, (w // 2) % 8, w % 2
    yc = y * 2 + c
    own_cols = pl.ds(pl.multiple_of(c * HALF, 128), HALF)
    other_cols = pl.ds(pl.multiple_of((1 - c) * HALF, 128), HALF)

    def wid(y_, z_, c_):
        return y_ * 16 + z_ * 2 + c_

    def rcopy(src, dst, ssem, rsem, w_, x_):
        return pltpu.make_async_remote_copy(
            src_ref=src, dst_ref=dst, send_sem=ssem, recv_sem=rsem,
            device_id=(w_, x_), device_id_type=MESH,
        )

    loads, held = [], []

    def load(src, dst):
        cp = pltpu.make_async_copy(src, dst, lsem.at[len(loads)])
        cp.start()
        loads.append(cp)
        held.append(cp)
        return cp

    def need(cp):
        held[:] = [h for h in held if h is not cp]
        cp.wait()

    drains = []

    def finish():
        for cp in held:
            cp.wait()
        for cond, cp in drains:
            if cond is None:
                cp.wait_send()
            else:
                @pl.when(cond)
                def _():
                    cp.wait_send()

    def send(cp, cond=None):
        if cond is None:
            cp.start()
        else:
            @pl.when(cond)
            def _():
                cp.start()

    def arrivals(ref, sem):
        rcopy(ref, ref, sem, sem, w, (x + 1) % 4).wait_recv()

    def drain(ref, sem, cond=None):
        drains.append((cond, rcopy(ref, ref, sem, sem, w, (x + 1) % 4)))

    bar = pltpu.get_barrier_semaphore()

    def greet(w_, x_):
        pl.semaphore_signal(bar, inc=1, device_id=(w_, x_), device_id_type=MESH)

    for k in (2, 1, 3):
        greet(w, (x + k) % 4)
    for k in (4, 5, 2, 3, 6, 7, 1):
        t = (yc + k) % 8
        greet(wid(t // 2, z, t % 2), x)
    for k in (1, 7):
        greet(wid(y, (z + k) % 8, c), x)
    l_slots = load(slots_h, slots)
    l_lengths = load(lengths_h, lengths)
    l_qn = load(qn_h, gq.at[yc, pl.ds(0, 2)])
    l_qr = load(qr_h, qr)
    l_ak = load(ak_h, ak)
    l_sv = load(slot_vec_h, slot_vec)
    l_gain = load(gain_h, gain_v)
    l_res = load(res_h, res)
    l_kv = load(kv_h, kv)
    l_av = load(av_h, av)
    l_wo = load(wo_h.at[:, own_cols], wo.at[0:128])
    l_wga = load(wg_h.at[:, own_cols], wga)
    l_wua = load(wu_h.at[:, own_cols], wua)
    l_wgb = load(wg_h.at[:, other_cols], wgb)
    l_wub = load(wu_h.at[:, other_cols], wub)
    l_wd = load(wd_h.at[:, own_cols], wd.at[0:288])

    pl.semaphore_wait(bar, 12)
    need(l_qr)
    gq[yc, 2] = jnp.concatenate([qr[0], qr[1]], axis=1)
    need(l_qn)
    for k in (4, 5, 2, 3, 6, 7, 1):
        t = (yc + k) % 8
        send(rcopy(gq.at[yc], gq.at[yc], ss_a.at[0], rs_a.at[0], wid(t // 2, z, t % 2), x))
    drain(gq.at[0:7], ss_a.at[0])
    partner = wid(y, z, 1 - c)
    send(rcopy(res_h.at[:, other_cols], resx, ss_w.at[0], rs_w.at[0], partner, x))
    send(rcopy(wo_h.at[:, other_cols], wo.at[128:256], ss_w.at[1], rs_w.at[1], partner, x))
    drain(resx, ss_w.at[0])
    drain(wo.at[128:256], ss_w.at[1])

    def hand_on(i):
        for k in (1, 7):
            pl.semaphore_signal(
                relay.at[i], inc=1, device_id=(wid(y, (z + k) % 8, c), x), device_id_type=MESH
            )

    hand_on(0)

    need(l_sv)
    sv = slot_vec[...]
    srow = (sv // 32) * 32 + ((sv // 2) & 1) * 16 + ((sv // 4) & 7) * 2 + (sv & 1)
    pm[...] = jnp.where(srow == iota((128, 128), 0), 1.0, 0.0).astype(BF)
    pl.semaphore_wait(relay.at[0], 2)
    hand_on(1)
    need(l_res)
    need(l_gain)
    gfull = gain_v[...].astype(F32).reshape(1, COLS)
    left, right = gfull[:, :HALF], gfull[:, HALF:]
    gain_own = jnp.where(c == 0, left, right)
    inv_own[...] = 1.0 / gain_own
    inv_other[...] = 1.0 / jnp.where(c == 0, right, left)
    for j in range(7):
        gains[j] = gain_own[:, 128 * j : 128 * j + 128]
    r32 = iota((32, 32), 0)
    c32 = iota((32, 32), 1)
    by_dest = jnp.where(c32 == (r32 & 1) * 16 + (r32 // 4) * 2 + ((r32 // 2) & 1), 1.0, 0.0).astype(BF)
    pl.semaphore_wait(relay.at[1], 2)
    hand_on(2)
    pl.semaphore_wait(relay.at[2], 2)

    arrivals(gq.at[0:7], rs_a.at[0])

    low = iota((16, 128), 1) < 64
    need(l_slots)
    need(l_lengths)
    for kz in FAR_FIRST + (0,):
        zt = (z + kz) % 8
        ropes = []
        for s in range(2):
            r = slots[wid(y, zt, c) * 2 + s]
            i8 = (r // 32) * 2 + ((r // 2) & 1)
            i = r & 1
            sq[zt, s] = gq[i8, i]
            tile = gq[i8, 2].astype(F32)
            ropes.append(jnp.where(i == s, tile, swap_halves(tile)))
        sq[zt, 2] = jnp.where(low, ropes[0], ropes[1]).astype(BF)
        if kz:
            send(rcopy(sq.at[zt], rq.at[z], ss_a.at[1], rs_a.at[1], wid(y, zt, c), x))
    drain(sq.at[0:7], ss_a.at[1])
    send(rcopy(wd_h.at[:, other_cols], wd.at[288:576], ss_w.at[2], rs_w.at[2], partner, x))
    drain(wd.at[288:576], ss_w.at[2])
    rq[z] = sq[z]
    arrivals(resx, rs_w.at[0])
    mine = jnp.where(c == 0, res[:, :HALF], res[:, HALF:]).astype(F32)
    theirs = resx[...].astype(F32)
    top = jnp.where(c == 0, mine, theirs)
    low2 = jnp.where(c == 0, theirs, mine)
    spread = jnp.concatenate([top] * 8 + [low2] * 8, axis=0)
    resmask[...] = jnp.where((iota((32, HALF), 0) // 2) % 8 == z, spread, 0.0)
    need(l_ak)
    need(l_kv)
    arrivals(rq.at[0:7], rs_a.at[1])

    q_parts, ropes = [], []
    for s in range(2):
        r = slots[w * 2 + s]
        zr = (r // 4) & 7
        q_parts.append(rq[zr, s])
        ropes.append(rq[zr, 2][:, 64 * s : 64 * s + 64])
    qn = jnp.concatenate(q_parts, axis=0)
    wide_q = jnp.concatenate([qn] * 16, axis=1)
    own_head = iota((32, 2048), 1) // 128 == (iota((32, 2048), 0) & 15)
    wide_q = jnp.where(own_head, wide_q, jnp.zeros_like(wide_q))
    qlat = dot(wide_q, ak[...].reshape(2048, 512)).astype(BF)
    ctxs = []
    for s in range(2):
        sc = dot(qlat[16 * s : 16 * s + 16], kv[s, 0:512])
        sc = (sc + dot(ropes[s], kv[s, 512:576])) * SCALE
        live = iota((16, 2048), 1) < lengths[s]
        sc = jnp.where(live, sc, -1e30)
        e = jnp.exp(sc - jnp.max(sc, axis=1, keepdims=True))
        e = jnp.where(live, e, 0.0)
        p = (e / jnp.sum(e, axis=1, keepdims=True)).astype(BF)
        ctxs.append(dot_nt(p, kv[s, 0:512]).astype(BF))
    ctx = jnp.concatenate(ctxs, axis=0)
    wide_c = jnp.concatenate([ctx] * 16, axis=1)
    own_head = iota((32, 8192), 1) // 512 == (iota((32, 8192), 0) & 15)
    wide_c = jnp.where(own_head, wide_c, jnp.zeros_like(wide_c))
    need(l_av)
    heads = dot(wide_c, av[...].reshape(8192, 128)).astype(BF)

    hp = dot(by_dest, heads)
    for zt in range(8):
        hs[zt] = hp[4 * zt : 4 * zt + 4].astype(BF)
    home = x == y
    for kz in FAR_FIRST + (0,):
        zt = (z + kz) % 8
        for kx in (2, 1, 3, 0):
            for kc in (1, 0):
                cp = rcopy(
                    hs.at[zt], hb.at[w], ss_c.at[0], rs_c.at[0],
                    wid(x, zt, (c + kc) % 2), (x + kx) % 4,
                )
                send(cp, x != y if kx == 0 and kz == 0 and kc == 0 else None)
    drain(hb.at[0:63], ss_c.at[0], home)
    drain(hb.at[0:64], ss_c.at[0], jnp.logical_not(home))

    @pl.when(home)
    def _():
        hb[w] = hs[z]
        arrivals(hb.at[0:63], rs_c.at[0])

    @pl.when(jnp.logical_not(home))
    def _():
        arrivals(hb.at[0:64], rs_c.at[0])

    for j in range(64):
        two = hb[j].astype(F32)
        hf[0, 2 * j : 2 * j + 2] = two[0:2]
        hf[1, 2 * j : 2 * j + 2] = two[2:4]
    need(l_wo)
    arrivals(wo.at[128:256], rs_w.at[1])
    both = jnp.concatenate([hf[c], hf[1 - c]], axis=1).astype(BF)
    heads_all = dot(pm[...], both).astype(BF)

    for g, (a, b) in enumerate(GROUPS):
        cols = slice(128 * a, 128 * b)
        part = dot(heads_all, wo[:, cols]).reshape(4, 32, -1)
        pown[:, :, cols] = part
        d1b[:, :, cols] = part.astype(BF)
        for k in (2, 1, 3):
            yt = (y + k) % 4
            send(rcopy(
                d1b.at[yt, :, cols], d1r.at[k - 1, :, cols], ss_d.at[0], rs_d.at[g],
                wid(yt, z, c), x,
            ))
    drain(d1b.at[0:3], ss_d.at[0])
    for g, (a, b) in enumerate(GROUPS):
        cols = slice(128 * a, 128 * b)
        total = pown[y, :, cols] + resmask[:, cols]
        arrivals(d1r.at[:, :, cols], rs_d.at[g])
        for k in range(3):
            total = total + d1r[k, :, cols].astype(F32)
        for j in range(a, b):
            piece = total[:, 128 * (j - a) : 128 * (j - a) + 128]
            asum[j] = piece
            d2b[j] = piece.astype(BF)
            k = (j + 8 - z) % 8
            send(rcopy(d2b.at[j], d2r.at[k], ss_z.at[0], rs_z.at[0], wid(y, j, c), x), z != j)
    drain(d2b.at[0:6], ss_z.at[0], z < 7)
    drain(d2b.at[0:7], ss_z.at[0], z == 7)

    zc = lax.min(z, 6)

    @pl.when(z < 7)
    def _():
        mid = asum[zc]
        arrivals(d2r.at[1:8], rs_z.at[0])
        for k in range(1, 8):
            mid = mid + d2r[k].astype(F32)
        f1[zc] = (mid * gains[zc]).astype(BF)

    zg = sum(jnp.where(zc >= b, 1, 0) for _, b in GROUPS[:-1])
    for k in FAR_FIRST:
        zt = (z + k) % 8
        send(rcopy(f1.at[zc], f1.at[zc], ss_f1.at[0], rs_f1.at[zg], wid(y, zt, c), x), z < 7)
    drain(f1.at[0:7], ss_f1.at[0], z < 7)

    sums = jnp.zeros((32, 1), F32)
    for g, (a, b) in enumerate(GROUPS):
        mine = jnp.logical_and(z >= a, z < b)

        @pl.when(jnp.logical_not(mine))
        def _():
            arrivals(f1.at[a:b], rs_f1.at[g])

        if b - a > 1:
            @pl.when(mine)
            def _():
                arrivals(f1.at[a : b - 1], rs_f1.at[g])

        cols = slice(128 * a, 128 * b)
        x16 = jnp.concatenate([f1[j] for j in range(a, b)], axis=1)
        f2[y, :, cols] = x16
        plain = x16.astype(F32) * inv_own[:, cols]
        sums = sums + jnp.sum(plain * plain, axis=1, keepdims=True)
        if g == NG - 1:
            high = sums.astype(BF).astype(F32)
            tag = jnp.where(iota((32, 128), 1) < 64, high, sums - high)
            f2[y, :, HALF : HALF + 128] = tag.astype(BF)
            cols = slice(128 * a, HALF + 128)
        for k in (2, 1, 3):
            yt = (y + k) % 4
            send(rcopy(
                f2.at[y, :, cols], f2.at[y, :, cols], ss_f2.at[0], rs_f2.at[g], wid(yt, z, c), x
            ))
        send(rcopy(
            f2.at[y, :, cols], f3.at[y, :, cols], ss_f2.at[1], rs_f3.at[g], wid(y, z, 1 - c), x
        ))
    drain(f2.at[0:3], ss_f2.at[0])
    drain(f2.at[0:4], ss_f2.at[1])

    need(l_wga)
    need(l_wua)

    def gate_up(acc, rows, w_gate, w_up, g):
        cols = slice(128 * GROUPS[g][0], 128 * GROUPS[g][1])
        act = rows[:, :, cols].reshape(128, -1)
        new = [dot_nt(act, w_gate[:, cols]), dot_nt(act, w_up[:, cols])]
        return new if acc is None else [p + q for p, q in zip(acc, new)]

    def span(g):
        a, b = GROUPS[g]
        return slice(128 * a, HALF + 128 if g == NG - 1 else 128 * b)

    acc = None
    for g in range(NG):
        arrivals(f2.at[0:3, :, span(g)], rs_f2.at[g])
        for k in (2, 1, 3):
            yb = (y + 4 - k) % 4
            send(rcopy(
                f2.at[yb, :, span(g)], f3.at[yb, :, span(g)], ss_f2.at[1], rs_f3.at[g],
                wid(y, z, 1 - c), x,
            ))
        acc = gate_up(acc, f2, wga, wua, g)
    need(l_wgb)
    need(l_wub)
    for g in range(NG):
        arrivals(f3.at[:, :, span(g)], rs_f3.at[g])
        acc = gate_up(acc, f3, wgb, wub, g)
    tags = f2[:, :, HALF:].reshape(128, 128).astype(F32) + f3[:, :, HALF:].reshape(128, 128).astype(F32)
    sums = tags[:, 0:1] + tags[:, 64:65]
    high = sums.astype(BF).astype(F32)
    tag = jnp.where(iota((128, 128), 1) < 64, high, sums - high).astype(BF)
    gate, up = acc[0].astype(BF), acc[1].astype(BF)
    for b in range(4):
        part = slice(32 * b, 32 * b + 32)
        g1b[b, :, 256:384] = tag[part]
        g1b[b, :, 640:768] = tag[part]
        g1b[b, :, 0:288] = gate[part]
        g1b[b, :, 384:672] = up[part]
    for k in (2, 1, 3):
        xt = (x + k) % 4
        send(rcopy(g1b.at[xt], g1r.at[k], ss_g.at[0], rs_g.at[0], w, xt))

    pick = jnp.where(iota((16, 32), 1) == c * 16 + z * 2 + iota((16, 32), 0), 1.0, 0.0).astype(BF)
    here = dot(pick, f2[y, :, 0:HALF])[0:2] * inv_own[...]
    there = dot(pick, f3[y, :, 0:HALF])[0:2] * inv_other[...]
    mrow[0] = here
    mrow[1] = there
    drain(g1b.at[0:3], ss_g.at[0])
    total = g1b[x].astype(F32)
    arrivals(g1r.at[1:4], rs_g.at[0])
    for k in range(1, 4):
        total = total + g1r[k].astype(F32)
    square = total[:, 288:289] + total[:, 320:321]
    norm = lax.rsqrt(square / D + 1e-06)
    gate = total[:, 0:288] * norm
    up = total[:, 384:672] * norm
    hid[0, x] = (gate / (1.0 + jnp.exp(-gate)) * up).astype(BF)
    for k in (2, 1, 3):
        xt = (x + k) % 4
        send(rcopy(hid.at[0, x], hid.at[1, x], ss_g.at[2], rs_g.at[2], partner, xt))
        send(rcopy(hid.at[0, x], hid.at[0, x], ss_g.at[1], rs_g.at[1], w, xt))
    send(rcopy(hid.at[0, x], hid.at[1, x], ss_g.at[2], rs_g.at[2], partner, x))
    drain(hid.at[0, 0:3], ss_g.at[1])
    drain(hid.at[1, 0:4], ss_g.at[2])
    need(l_wd)
    arrivals(wd.at[288:576], rs_w.at[2])
    arrivals(hid.at[0, 0:3], rs_g.at[1])
    arrivals(hid.at[1, 0:4], rs_g.at[2])

    near = hid[0].reshape(128, 288)
    far = hid[1].reshape(128, 288)
    for g, (a, b) in enumerate(GROUPS):
        cols = slice(128 * a, 128 * b)
        part = (dot(near, wd[0:288, cols]) + dot(far, wd[288:576, cols])).reshape(4, 32, -1)
        pown2[:, :, cols] = part
        h1b[:, :, cols] = part.astype(BF)
        for k in (2, 1, 3):
            yt = (y + k) % 4
            send(rcopy(
                h1b.at[yt, :, cols], h1r.at[k - 1, :, cols], ss_h.at[0], rs_h.at[g],
                wid(yt, z, c), x,
            ))
    drain(h1b.at[0:3], ss_h.at[0])
    for g, (a, b) in enumerate(GROUPS):
        cols = slice(128 * a, 128 * b)
        total = pown2[y, :, cols]
        arrivals(h1r.at[:, :, cols], rs_h.at[g])
        for k in range(3):
            total = total + h1r[k, :, cols].astype(F32)
        for j in range(16):
            piece = total[2 * j : 2 * j + 2]
            h2f[j, :, cols] = piece
            h2b[j, :, cols] = piece.astype(BF)
        for n, (first, last) in enumerate(LAST):
            if last != g:
                continue
            cols = slice(128 * GROUPS[first][0], 128 * b)
            for kz in FAR_FIRST + (0,):
                for kc in (1, 0):
                    if kz or kc:
                        zt, ct = (z + kz) % 8, (c + kc) % 2
                        send(rcopy(
                            h2b.at[ct * 8 + zt, :, cols], h2r.at[kc * 8 + kz, :, cols],
                            ss_o.at[0], rs_o.at[n], wid(y, zt, ct), x,
                        ))
    drain(h2b.at[0:15], ss_o.at[0])
    for n, (first, last) in enumerate(LAST):
        a, b = GROUPS[first][0], GROUPS[last][1]
        cols = slice(128 * a, 128 * b)
        mine = mrow[0, :, cols] + h2f[c * 8 + z, :, cols]
        theirs = mrow[1, :, cols]
        arrivals(h2r.at[1:16, :, cols], rs_o.at[n])
        for k in range(8):
            if k:
                mine = mine + h2r[k, :, cols].astype(F32)
            theirs = theirs + h2r[8 + k, :, cols].astype(F32)
        out[:, cols] = jnp.where(c == 0, mine, theirs).astype(BF)
        right = slice(HALF + 128 * a, HALF + 128 * b)
        out[:, right] = jnp.where(c == 0, theirs, mine).astype(BF)

    finish()


def shards(
    residual_in, query_nope, query_rope, absorb_key, absorb_value, latent_cache, cache_lengths,
    slot_rows, out_proj, norm_gain, gate_weight, up_weight, down_weight,
):
    v = pltpu.VMEM
    sem = pltpu.SemaphoreType.DMA
    scratch = [
        pltpu.SMEM((128,), jnp.int32), pltpu.SMEM((2,), jnp.int32),
        v((1, 128), jnp.int32), v((COLS,), BF), v((2, COLS), BF), v((2, 16, 64), BF),
        v((16, 128, 512), BF), v((16, 512, 128), BF), v((2, 576, 2048), BF), v((256, HALF), BF),
        v((288, HALF), BF), v((288, HALF), BF), v((288, HALF), BF), v((288, HALF), BF),
        v((576, HALF), BF), sem((16,)),
        pltpu.SemaphoreType.REGULAR((3,)),
        v((8, 3, 16, 128), BF), v((8, 3, 16, 128), BF), v((8, 3, 16, 128), BF), sem((2,)), sem((2,)),
        v((8, 4, 128), BF), v((64, 4, 128), BF), v((2, 128, 128), F32), sem((1,)), sem((1,)),
        v((128, 128), BF), v((7, 1, 128), F32), v((1, HALF), F32), v((1, HALF), F32),
        v((2, HALF), BF), v((32, HALF), F32), sem((3,)), sem((3,)),
        v((4, 32, HALF), F32), v((4, 32, HALF), BF), v((3, 32, HALF), BF), sem((1,)), sem((NG,)),
        v((7, 32, 128), F32), v((7, 32, 128), BF), v((8, 32, 128), BF), sem((1,)), sem((1,)),
        v((7, 32, 128), BF), v((4, 32, HALF + 128), BF), v((4, 32, HALF + 128), BF),
        v((2, 2, HALF), F32), sem((1,)), sem((NG,)), sem((2,)), sem((NG,)), sem((NG,)),
        v((4, 32, 768), BF), v((4, 32, 768), BF), v((2, 4, 32, 288), BF), sem((3,)), sem((3,)),
        v((4, 32, HALF), F32), v((4, 32, HALF), BF), v((3, 32, HALF), BF), sem((1,)), sem((NG,)),
        v((16, 2, HALF), BF), v((16, 2, HALF), F32), v((16, 2, HALF), BF), sem((1,)), sem((len(LAST),)),
    ]
    return pl.pallas_call(
        kernel,
        out_shape=jax.ShapeDtypeStruct((2, COLS), BF),
        in_specs=[HBM] * 14,
        out_specs=VM,
        scratch_shapes=scratch,
        compiler_params=pltpu.CompilerParams(
            collective_id=0, has_side_effects=True, vmem_limit_bytes=67043328
        ),
    )(
        slot_rows, cache_lengths, slot_rows.reshape(1, 128), norm_gain,
        residual_in, query_nope, query_rope, absorb_key, absorb_value,
        jnp.swapaxes(latent_cache, 1, 2), out_proj, gate_weight.T, up_weight.T, down_weight,
    )


def solution(mesh):
    in_specs = (
        P("wide", "narrow"),
        P("wide", "narrow", None),
        P("wide", "narrow", None),
        P("narrow", None, None),
        P("narrow", None, None),
        P("wide", None, None),
        P("wide"),
        P(),
        P("wide", "narrow"),
        P("narrow"),
        P("narrow", "wide"),
        P("narrow", "wide"),
        P("wide", "narrow"),
    )
    out_specs = P("wide", "narrow")
    return jax.shard_map(shards, mesh=mesh, in_specs=in_specs, out_specs=out_specs, check_vma=False)
```

```python
import math

import jax
import jax.numpy as jnp
from jax import lax
from jax.experimental import pallas as pl
from jax.experimental.pallas import tpu as pltpu
from jax.sharding import PartitionSpec as P

D = 7168
MESH = pl.DeviceIdType.MESH
F32 = jnp.float32
BF = jnp.bfloat16
COLS = 1792
HALF = COLS // 2
GROUPS = ((0, 2), (2, 4), (4, 6), (6, 7))
NG = len(GROUPS)
LAST = ((0, 1), (2, 3))
FAR_FIRST = (4, 3, 5, 2, 6, 1, 7)
SCALE = 1.0 / math.sqrt(192)
HBM = pl.BlockSpec(memory_space=pltpu.HBM)
VM = pl.BlockSpec(memory_space=pltpu.VMEM)


def dot(a, b):
    return jnp.dot(a, b, preferred_element_type=F32)


def dot_nt(a, b):
    return lax.dot_general(a, b, (((1,), (1,)), ((), ())), preferred_element_type=F32)


def iota(shape, axis):
    return lax.broadcasted_iota(jnp.int32, shape, axis)


def swap_halves(tile):
    return jnp.concatenate([tile[:, 64:], tile[:, :64]], axis=1)


def kernel(
    slots_h, lengths_h, slot_vec_h, gain_h,
    res_h, qn_h, qr_h, ak_h, av_h, kv_h, wo_h, wg_h, wu_h, wd_h,
    out,
    slots, lengths, slot_vec, gain_v, res, qr, ak, av, kv, wo, wga, wgb, wua, wub, wd, lsem,
    relay, gq, sq, rq, ss_a, rs_a, hs, hb, hf, ss_c, rs_c,
    pm, gains, inv_own, inv_other, resx, resmask, ss_w, rs_w,
    pown, d1b, d1r, ss_d, rs_d, asum, d2b, d2r, ss_z, rs_z,
    f1, f2, f3, mrow, ss_f1, rs_f1, ss_f2, rs_f2, rs_f3,
    g1b, g1r, hid, ss_g, rs_g,
    pown2, h1b, h1r, ss_h, rs_h, h2b, h2f, h2r, ss_o, rs_o,
):
    w = lax.axis_index("wide")
    x = lax.axis_index("narrow")
    y, z, c = w // 16, (w // 2) % 8, w % 2
    yc = y * 2 + c
    own_cols = pl.ds(pl.multiple_of(c * HALF, 128), HALF)
    other_cols = pl.ds(pl.multiple_of((1 - c) * HALF, 128), HALF)

    def wid(y_, z_, c_):
        return y_ * 16 + z_ * 2 + c_

    def rcopy(src, dst, ssem, rsem, w_, x_):
        return pltpu.make_async_remote_copy(
            src_ref=src, dst_ref=dst, send_sem=ssem, recv_sem=rsem,
            device_id=(w_, x_), device_id_type=MESH,
        )

    loads, held = [], []

    def load(src, dst):
        cp = pltpu.make_async_copy(src, dst, lsem.at[len(loads)])
        cp.start()
        loads.append(cp)
        held.append(cp)
        return cp

    def need(cp):
        held[:] = [h for h in held if h is not cp]
        cp.wait()

    drains = []

    def finish():
        for cp in held:
            cp.wait()
        for cond, cp in drains:
            if cond is None:
                cp.wait_send()
            else:
                @pl.when(cond)
                def _():
                    cp.wait_send()

    def send(cp, cond=None):
        if cond is None:
            cp.start()
        else:
            @pl.when(cond)
            def _():
                cp.start()

    def arrivals(ref, sem):
        rcopy(ref, ref, sem, sem, w, (x + 1) % 4).wait_recv()

    def drain(ref, sem, cond=None):
        drains.append((cond, rcopy(ref, ref, sem, sem, w, (x + 1) % 4)))

    bar = pltpu.get_barrier_semaphore()

    def greet(w_, x_):
        pl.semaphore_signal(bar, inc=1, device_id=(w_, x_), device_id_type=MESH)

    for k in (2, 1, 3):
        greet(w, (x + k) % 4)
    for k in (4, 5, 2, 3, 6, 7, 1):
        t = (yc + k) % 8
        greet(wid(t // 2, z, t % 2), x)
    for k in (1, 7):
        greet(wid(y, (z + k) % 8, c), x)
    l_slots = load(slots_h, slots)
    l_lengths = load(lengths_h, lengths)
    l_qn = load(qn_h, gq.at[yc, pl.ds(0, 2)])
    l_qr = load(qr_h, qr)
    l_ak = load(ak_h, ak)
    l_sv = load(slot_vec_h, slot_vec)
    l_gain = load(gain_h, gain_v)
    l_res = load(res_h, res)
    l_kv = load(kv_h, kv)
    l_av = load(av_h, av)
    l_wo = load(wo_h.at[:, own_cols], wo.at[0:128])
    l_wga = load(wg_h.at[:, own_cols], wga)
    l_wua = load(wu_h.at[:, own_cols], wua)
    l_wgb = load(wg_h.at[:, other_cols], wgb)
    l_wub = load(wu_h.at[:, other_cols], wub)
    l_wd = load(wd_h.at[:, own_cols], wd.at[0:288])

    pl.semaphore_wait(bar, 12)
    need(l_qr)
    gq[yc, 2] = jnp.concatenate([qr[0], qr[1]], axis=1)
    need(l_qn)
    for k in (4, 5, 2, 3, 6, 7, 1):
        t = (yc + k) % 8
        send(rcopy(gq.at[yc], gq.at[yc], ss_a.at[0], rs_a.at[0], wid(t // 2, z, t % 2), x))
    drain(gq.at[0:7], ss_a.at[0])
    partner = wid(y, z, 1 - c)
    send(rcopy(res_h.at[:, other_cols], resx, ss_w.at[0], rs_w.at[0], partner, x))
    send(rcopy(wo_h.at[:, other_cols], wo.at[128:256], ss_w.at[1], rs_w.at[1], partner, x))
    drain(resx, ss_w.at[0])
    drain(wo.at[128:256], ss_w.at[1])

    def hand_on(i):
        for k in (1, 7):
            pl.semaphore_signal(
                relay.at[i], inc=1, device_id=(wid(y, (z + k) % 8, c), x), device_id_type=MESH
            )

    hand_on(0)

    need(l_sv)
    sv = slot_vec[...]
    srow = (sv // 32) * 32 + ((sv // 2) & 1) * 16 + ((sv // 4) & 7) * 2 + (sv & 1)
    pm[...] = jnp.where(srow == iota((128, 128), 0), 1.0, 0.0).astype(BF)
    pl.semaphore_wait(relay.at[0], 2)
    hand_on(1)
    need(l_res)
    need(l_gain)
    gfull = gain_v[...].astype(F32).reshape(1, COLS)
    left, right = gfull[:, :HALF], gfull[:, HALF:]
    gain_own = jnp.where(c == 0, left, right)
    inv_own[...] = 1.0 / gain_own
    inv_other[...] = 1.0 / jnp.where(c == 0, right, left)
    for j in range(7):
        gains[j] = gain_own[:, 128 * j : 128 * j + 128]
    r32 = iota((32, 32), 0)
    c32 = iota((32, 32), 1)
    by_dest = jnp.where(c32 == (r32 & 1) * 16 + (r32 // 4) * 2 + ((r32 // 2) & 1), 1.0, 0.0).astype(BF)
    pl.semaphore_wait(relay.at[1], 2)
    hand_on(2)
    pl.semaphore_wait(relay.at[2], 2)

    arrivals(gq.at[0:7], rs_a.at[0])

    low = iota((16, 128), 1) < 64
    need(l_slots)
    need(l_lengths)
    for kz in FAR_FIRST + (0,):
        zt = (z + kz) % 8
        ropes = []
        for s in range(2):
            r = slots[wid(y, zt, c) * 2 + s]
            i8 = (r // 32) * 2 + ((r // 2) & 1)
            i = r & 1
            sq[zt, s] = gq[i8, i]
            tile = gq[i8, 2].astype(F32)
            ropes.append(jnp.where(i == s, tile, swap_halves(tile)))
        sq[zt, 2] = jnp.where(low, ropes[0], ropes[1]).astype(BF)
        if kz:
            send(rcopy(sq.at[zt], rq.at[z], ss_a.at[1], rs_a.at[1], wid(y, zt, c), x))
    drain(sq.at[0:7], ss_a.at[1])
    send(rcopy(wd_h.at[:, other_cols], wd.at[288:576], ss_w.at[2], rs_w.at[2], partner, x))
    drain(wd.at[288:576], ss_w.at[2])
    rq[z] = sq[z]
    arrivals(resx, rs_w.at[0])
    mine = jnp.where(c == 0, res[:, :HALF], res[:, HALF:]).astype(F32)
    theirs = resx[...].astype(F32)
    top = jnp.where(c == 0, mine, theirs)
    low2 = jnp.where(c == 0, theirs, mine)
    spread = jnp.concatenate([top] * 8 + [low2] * 8, axis=0)
    resmask[...] = jnp.where((iota((32, HALF), 0) // 2) % 8 == z, spread, 0.0)
    need(l_ak)
    need(l_kv)
    arrivals(rq.at[0:7], rs_a.at[1])

    q_parts, ropes = [], []
    for s in range(2):
        r = slots[w * 2 + s]
        zr = (r // 4) & 7
        q_parts.append(rq[zr, s])
        ropes.append(rq[zr, 2][:, 64 * s : 64 * s + 64])
    qn = jnp.concatenate(q_parts, axis=0)
    wide_q = jnp.concatenate([qn] * 16, axis=1)
    own_head = iota((32, 2048), 1) // 128 == (iota((32, 2048), 0) & 15)
    wide_q = jnp.where(own_head, wide_q, jnp.zeros_like(wide_q))
    qlat = dot(wide_q, ak[...].reshape(2048, 512)).astype(BF)
    ctxs = []
    for s in range(2):
        sc = dot(qlat[16 * s : 16 * s + 16], kv[s, 0:512])
        sc = (sc + dot(ropes[s], kv[s, 512:576])) * SCALE
        live = iota((16, 2048), 1) < lengths[s]
        sc = jnp.where(live, sc, -1e30)
        e = jnp.exp(sc - jnp.max(sc, axis=1, keepdims=True))
        e = jnp.where(live, e, 0.0)
        p = (e / jnp.sum(e, axis=1, keepdims=True)).astype(BF)
        ctxs.append(dot_nt(p, kv[s, 0:512]).astype(BF))
    ctx = jnp.concatenate(ctxs, axis=0)
    wide_c = jnp.concatenate([ctx] * 16, axis=1)
    own_head = iota((32, 8192), 1) // 512 == (iota((32, 8192), 0) & 15)
    wide_c = jnp.where(own_head, wide_c, jnp.zeros_like(wide_c))
    need(l_av)
    heads = dot(wide_c, av[...].reshape(8192, 128)).astype(BF)

    hp = dot(by_dest, heads)
    for zt in range(8):
        hs[zt] = hp[4 * zt : 4 * zt + 4].astype(BF)
    home = x == y
    for kz in FAR_FIRST + (0,):
        zt = (z + kz) % 8
        for kx in (2, 1, 3, 0):
            for kc in (1, 0):
                cp = rcopy(
                    hs.at[zt], hb.at[w], ss_c.at[0], rs_c.at[0],
                    wid(x, zt, (c + kc) % 2), (x + kx) % 4,
                )
                send(cp, x != y if kx == 0 and kz == 0 and kc == 0 else None)
    drain(hb.at[0:63], ss_c.at[0], home)
    drain(hb.at[0:64], ss_c.at[0], jnp.logical_not(home))

    @pl.when(home)
    def _():
        hb[w] = hs[z]
        arrivals(hb.at[0:63], rs_c.at[0])

    @pl.when(jnp.logical_not(home))
    def _():
        arrivals(hb.at[0:64], rs_c.at[0])

    for j in range(64):
        two = hb[j].astype(F32)
        hf[0, 2 * j : 2 * j + 2] = two[0:2]
        hf[1, 2 * j : 2 * j + 2] = two[2:4]
    need(l_wo)
    arrivals(wo.at[128:256], rs_w.at[1])
    both = jnp.concatenate([hf[c], hf[1 - c]], axis=1).astype(BF)
    heads_all = dot(pm[...], both).astype(BF)

    for g, (a, b) in enumerate(GROUPS):
        cols = slice(128 * a, 128 * b)
        part = dot(heads_all, wo[:, cols]).reshape(4, 32, -1)
        pown[:, :, cols] = part
        d1b[:, :, cols] = part.astype(BF)
        for k in (2, 1, 3):
            yt = (y + k) % 4
            send(rcopy(
                d1b.at[yt, :, cols], d1r.at[k - 1, :, cols], ss_d.at[0], rs_d.at[g],
                wid(yt, z, c), x,
            ))
    drain(d1b.at[0:3], ss_d.at[0])
    for g, (a, b) in enumerate(GROUPS):
        cols = slice(128 * a, 128 * b)
        total = pown[y, :, cols] + resmask[:, cols]
        arrivals(d1r.at[:, :, cols], rs_d.at[g])
        for k in range(3):
            total = total + d1r[k, :, cols].astype(F32)
        for j in range(a, b):
            piece = total[:, 128 * (j - a) : 128 * (j - a) + 128]
            asum[j] = piece
            d2b[j] = piece.astype(BF)
            k = (j + 8 - z) % 8
            send(rcopy(d2b.at[j], d2r.at[k], ss_z.at[0], rs_z.at[0], wid(y, j, c), x), z != j)
    drain(d2b.at[0:6], ss_z.at[0], z < 7)
    drain(d2b.at[0:7], ss_z.at[0], z == 7)

    zc = lax.min(z, 6)

    @pl.when(z < 7)
    def _():
        mid = asum[zc]
        arrivals(d2r.at[1:8], rs_z.at[0])
        for k in range(1, 8):
            mid = mid + d2r[k].astype(F32)
        f1[zc] = (mid * gains[zc]).astype(BF)

    zg = sum(jnp.where(zc >= b, 1, 0) for _, b in GROUPS[:-1])
    for k in FAR_FIRST:
        zt = (z + k) % 8
        send(rcopy(f1.at[zc], f1.at[zc], ss_f1.at[0], rs_f1.at[zg], wid(y, zt, c), x), z < 7)
    drain(f1.at[0:7], ss_f1.at[0], z < 7)

    sums = jnp.zeros((32, 1), F32)
    for g, (a, b) in enumerate(GROUPS):
        mine = jnp.logical_and(z >= a, z < b)

        @pl.when(jnp.logical_not(mine))
        def _():
            arrivals(f1.at[a:b], rs_f1.at[g])

        if b - a > 1:
            @pl.when(mine)
            def _():
                arrivals(f1.at[a : b - 1], rs_f1.at[g])

        cols = slice(128 * a, 128 * b)
        x16 = jnp.concatenate([f1[j] for j in range(a, b)], axis=1)
        f2[y, :, cols] = x16
        plain = x16.astype(F32) * inv_own[:, cols]
        sums = sums + jnp.sum(plain * plain, axis=1, keepdims=True)
        if g == NG - 1:
            high = sums.astype(BF).astype(F32)
            tag = jnp.where(iota((32, 128), 1) < 64, high, sums - high)
            f2[y, :, HALF : HALF + 128] = tag.astype(BF)
            cols = slice(128 * a, HALF + 128)
        for k in (2, 1, 3):
            yt = (y + k) % 4
            send(rcopy(
                f2.at[y, :, cols], f2.at[y, :, cols], ss_f2.at[0], rs_f2.at[g], wid(yt, z, c), x
            ))
        send(rcopy(
            f2.at[y, :, cols], f3.at[y, :, cols], ss_f2.at[1], rs_f3.at[g], wid(y, z, 1 - c), x
        ))
    drain(f2.at[0:3], ss_f2.at[0])
    drain(f2.at[0:4], ss_f2.at[1])

    need(l_wga)
    need(l_wua)

    def gate_up(acc, rows, w_gate, w_up, g):
        cols = slice(128 * GROUPS[g][0], 128 * GROUPS[g][1])
        act = rows[:, :, cols].reshape(128, -1)
        new = [dot_nt(act, w_gate[:, cols]), dot_nt(act, w_up[:, cols])]
        return new if acc is None else [p + q for p, q in zip(acc, new)]

    def span(g):
        a, b = GROUPS[g]
        return slice(128 * a, HALF + 128 if g == NG - 1 else 128 * b)

    acc = None
    for g in range(NG):
        arrivals(f2.at[0:3, :, span(g)], rs_f2.at[g])
        for k in (2, 1, 3):
            yb = (y + 4 - k) % 4
            send(rcopy(
                f2.at[yb, :, span(g)], f3.at[yb, :, span(g)], ss_f2.at[1], rs_f3.at[g],
                wid(y, z, 1 - c), x,
            ))
        acc = gate_up(acc, f2, wga, wua, g)
    need(l_wgb)
    need(l_wub)
    for g in range(NG):
        arrivals(f3.at[:, :, span(g)], rs_f3.at[g])
        acc = gate_up(acc, f3, wgb, wub, g)
    tags = f2[:, :, HALF:].reshape(128, 128).astype(F32) + f3[:, :, HALF:].reshape(128, 128).astype(F32)
    sums = tags[:, 0:1] + tags[:, 64:65]
    high = sums.astype(BF).astype(F32)
    tag = jnp.where(iota((128, 128), 1) < 64, high, sums - high).astype(BF)
    gate, up = acc[0].astype(BF), acc[1].astype(BF)
    for b in range(4):
        part = slice(32 * b, 32 * b + 32)
        g1b[b, :, 256:384] = tag[part]
        g1b[b, :, 640:768] = tag[part]
        g1b[b, :, 0:288] = gate[part]
        g1b[b, :, 384:672] = up[part]
        k = (b + 4 - x) % 4
        send(rcopy(g1b.at[b], g1r.at[k], ss_g.at[0], rs_g.at[0], w, b), x != b)

    pick = jnp.where(iota((16, 32), 1) == c * 16 + z * 2 + iota((16, 32), 0), 1.0, 0.0).astype(BF)
    here = dot(pick, f2[y, :, 0:HALF])[0:2] * inv_own[...]
    there = dot(pick, f3[y, :, 0:HALF])[0:2] * inv_other[...]
    mrow[0] = here
    mrow[1] = there
    drain(g1b.at[0:3], ss_g.at[0])
    total = g1b[x].astype(F32)
    arrivals(g1r.at[1:4], rs_g.at[0])
    for k in range(1, 4):
        total = total + g1r[k].astype(F32)
    square = total[:, 288:289] + total[:, 320:321]
    norm = lax.rsqrt(square / D + 1e-06)
    gate = total[:, 0:288] * norm
    up = total[:, 384:672] * norm
    hid[0, x] = (gate / (1.0 + jnp.exp(-gate)) * up).astype(BF)
    for k in (2, 1, 3):
        xt = (x + k) % 4
        send(rcopy(hid.at[0, x], hid.at[1, x], ss_g.at[2], rs_g.at[2], partner, xt))
        send(rcopy(hid.at[0, x], hid.at[0, x], ss_g.at[1], rs_g.at[1], w, xt))
    send(rcopy(hid.at[0, x], hid.at[1, x], ss_g.at[2], rs_g.at[2], partner, x))
    drain(hid.at[0, 0:3], ss_g.at[1])
    drain(hid.at[1, 0:4], ss_g.at[2])
    need(l_wd)
    arrivals(wd.at[288:576], rs_w.at[2])
    arrivals(hid.at[0, 0:3], rs_g.at[1])
    arrivals(hid.at[1, 0:4], rs_g.at[2])

    near = hid[0].reshape(128, 288)
    far = hid[1].reshape(128, 288)
    for g, (a, b) in enumerate(GROUPS):
        cols = slice(128 * a, 128 * b)
        part = (dot(near, wd[0:288, cols]) + dot(far, wd[288:576, cols])).reshape(4, 32, -1)
        pown2[:, :, cols] = part
        h1b[:, :, cols] = part.astype(BF)
        for k in (2, 1, 3):
            yt = (y + k) % 4
            send(rcopy(
                h1b.at[yt, :, cols], h1r.at[k - 1, :, cols], ss_h.at[0], rs_h.at[g],
                wid(yt, z, c), x,
            ))
    drain(h1b.at[0:3], ss_h.at[0])
    for g, (a, b) in enumerate(GROUPS):
        cols = slice(128 * a, 128 * b)
        total = pown2[y, :, cols]
        arrivals(h1r.at[:, :, cols], rs_h.at[g])
        for k in range(3):
            total = total + h1r[k, :, cols].astype(F32)
        for j in range(16):
            piece = total[2 * j : 2 * j + 2]
            h2f[j, :, cols] = piece
            h2b[j, :, cols] = piece.astype(BF)
        for n, (first, last) in enumerate(LAST):
            if last != g:
                continue
            cols = slice(128 * GROUPS[first][0], 128 * b)
            for kz in FAR_FIRST + (0,):
                for kc in (1, 0):
                    if kz or kc:
                        zt, ct = (z + kz) % 8, (c + kc) % 2
                        send(rcopy(
                            h2b.at[ct * 8 + zt, :, cols], h2r.at[kc * 8 + kz, :, cols],
                            ss_o.at[0], rs_o.at[n], wid(y, zt, ct), x,
                        ))
    drain(h2b.at[0:15], ss_o.at[0])
    for n, (first, last) in enumerate(LAST):
        a, b = GROUPS[first][0], GROUPS[last][1]
        cols = slice(128 * a, 128 * b)
        mine = mrow[0, :, cols] + h2f[c * 8 + z, :, cols]
        theirs = mrow[1, :, cols]
        arrivals(h2r.at[1:16, :, cols], rs_o.at[n])
        for k in range(8):
            if k:
                mine = mine + h2r[k, :, cols].astype(F32)
            theirs = theirs + h2r[8 + k, :, cols].astype(F32)
        out[:, cols] = jnp.where(c == 0, mine, theirs).astype(BF)
        right = slice(HALF + 128 * a, HALF + 128 * b)
        out[:, right] = jnp.where(c == 0, theirs, mine).astype(BF)

    finish()


def shards(
    residual_in, query_nope, query_rope, absorb_key, absorb_value, latent_cache, cache_lengths,
    slot_rows, out_proj, norm_gain, gate_weight, up_weight, down_weight,
):
    v = pltpu.VMEM
    sem = pltpu.SemaphoreType.DMA
    scratch = [
        pltpu.SMEM((128,), jnp.int32), pltpu.SMEM((2,), jnp.int32),
        v((1, 128), jnp.int32), v((COLS,), BF), v((2, COLS), BF), v((2, 16, 64), BF),
        v((16, 128, 512), BF), v((16, 512, 128), BF), v((2, 576, 2048), BF), v((256, HALF), BF),
        v((288, HALF), BF), v((288, HALF), BF), v((288, HALF), BF), v((288, HALF), BF),
        v((576, HALF), BF), sem((16,)),
        pltpu.SemaphoreType.REGULAR((3,)),
        v((8, 3, 16, 128), BF), v((8, 3, 16, 128), BF), v((8, 3, 16, 128), BF), sem((2,)), sem((2,)),
        v((8, 4, 128), BF), v((64, 4, 128), BF), v((2, 128, 128), F32), sem((1,)), sem((1,)),
        v((128, 128), BF), v((7, 1, 128), F32), v((1, HALF), F32), v((1, HALF), F32),
        v((2, HALF), BF), v((32, HALF), F32), sem((3,)), sem((3,)),
        v((4, 32, HALF), F32), v((4, 32, HALF), BF), v((3, 32, HALF), BF), sem((1,)), sem((NG,)),
        v((7, 32, 128), F32), v((7, 32, 128), BF), v((8, 32, 128), BF), sem((1,)), sem((1,)),
        v((7, 32, 128), BF), v((4, 32, HALF + 128), BF), v((4, 32, HALF + 128), BF),
        v((2, 2, HALF), F32), sem((1,)), sem((NG,)), sem((2,)), sem((NG,)), sem((NG,)),
        v((4, 32, 768), BF), v((4, 32, 768), BF), v((2, 4, 32, 288), BF), sem((3,)), sem((3,)),
        v((4, 32, HALF), F32), v((4, 32, HALF), BF), v((3, 32, HALF), BF), sem((1,)), sem((NG,)),
        v((16, 2, HALF), BF), v((16, 2, HALF), F32), v((16, 2, HALF), BF), sem((1,)), sem((len(LAST),)),
    ]
    return pl.pallas_call(
        kernel,
        out_shape=jax.ShapeDtypeStruct((2, COLS), BF),
        in_specs=[HBM] * 14,
        out_specs=VM,
        scratch_shapes=scratch,
        compiler_params=pltpu.CompilerParams(
            collective_id=0, has_side_effects=True, vmem_limit_bytes=67043328
        ),
    )(
        slot_rows, cache_lengths, slot_rows.reshape(1, 128), norm_gain,
        residual_in, query_nope, query_rope, absorb_key, absorb_value,
        jnp.swapaxes(latent_cache, 1, 2), out_proj, gate_weight.T, up_weight.T, down_weight,
    )


def solution(mesh):
    in_specs = (
        P("wide", "narrow"),
        P("wide", "narrow", None),
        P("wide", "narrow", None),
        P("narrow", None, None),
        P("narrow", None, None),
        P("wide", None, None),
        P("wide"),
        P(),
        P("wide", "narrow"),
        P("narrow"),
        P("narrow", "wide"),
        P("narrow", "wide"),
        P("wide", "narrow"),
    )
    out_specs = P("wide", "narrow")
    return jax.shard_map(shards, mesh=mesh, in_specs=in_specs, out_specs=out_specs, check_vma=False)
```
